512 devices in a mesh: cell: 64 (over z, y), help: 8 (over x, core).
Axes of the slice: x: 4, y: 4, z: 16, core: 2. Of those that a mesh axis runs over, the one named last changes fastest.
Arguments:
- weights: float32 [64, 896, 896], P('cell', 'help'), may hold values from 1 to 4096
- counts: int32 [64], P('cell'), may hold values from 224 to 896, as said below
- select: int32 [64, 128], P('cell'), may hold values from 0 to 895, as said below
- cut_weights: bfloat16 [64, 128, 8192], P('cell', 'help'), may hold values from 1 to 256
Outputs:
- parent_rows: float32 [64, 128, 8192], P('cell', 'help')
The draws below stay inside these ranges and needn't reach their ends.
Inputs may be any that keep to these rules, and one draw needn't show every extreme that they name: `counts`: one cell's count is exactly 896. `select`: each row holds 128 distinct vertex numbers of its cell, each below that cell's count.
All inputs are finite; a program needn't handle non-finite values.
Results may differ from the reference program's by a relative error of at most 0.0003.
Values sent between devices are 32-bit elements; how exact they have to be, the bound alone decides.
A program may use at most 64 MiB of HBM per device.

```python
import jax
import jax.numpy as jnp
from jax import lax

CAP = 896
PB = 128
SQUARINGS = 2
CELLS = 64


def boundary_layout(key):
    folded = jax.random.fold_in(key, 7)
    first_key, second_key, third_key = jax.random.split(folded, 3)
    counts = jax.random.randint(first_key, (CELLS,), CAP // 4, CAP + 1, dtype=jnp.int32)
    heaviest = jax.random.randint(second_key, (), 0, CELLS, dtype=jnp.int32)
    counts = jnp.where(jnp.arange(CELLS, dtype=jnp.int32) == heaviest, CAP, counts)
    positions = jnp.arange(CAP, dtype=jnp.int32)
    scores = jax.random.randint(third_key, (CELLS, CAP), 0, 1 << 20, dtype=jnp.int32) * CAP + positions[None, :]
    scores = jnp.where(positions[None, :] >= counts[:, None], scores + (1 << 30), scores)
    ranking = jnp.argsort(scores, axis=1, stable=True)[:, :PB].astype(jnp.int32)
    return (counts, ranking)


def draw_counts(key, part):
    counts, ranking = boundary_layout(key)
    return counts


def draw_select(key, part):
    counts, ranking = boundary_layout(key)
    return ranking


def draw_weights(key, part):
    folded = jax.random.fold_in(key, 11)
    first_key, second_key = jax.random.split(folded, 2)
    trapped = jax.random.randint(first_key, (CELLS, CAP), 0, 4, dtype=jnp.int32) == 0
    fraction = jax.random.uniform(second_key, (CELLS, CAP, CAP), jnp.float32)
    middle = 32.0 + 4064.0 * fraction
    light = 1.0 + 31.0 * fraction
    heavy = 3968.0 + 128.0 * fraction
    values = jnp.where(trapped[:, :, None], heavy, jnp.where(trapped[:, None, :], light, middle))
    return jnp.clip(values, 1.0, 4096.0).astype(jnp.float32)


def draw_cut_weights(key, part):
    folded = jax.random.fold_in(key, 13)
    values = jax.random.randint(folded, (CELLS, PB, CELLS * PB), 1, 256, dtype=jnp.int32).astype(jnp.float32)
    return values.astype(jnp.bfloat16)


def setup_inputs(seed: int = 0) -> dict:
    splits = jax.random.split(jax.random.key(seed), 5)
    return {
        "weights": draw_weights(jax.random.fold_in(splits[4], 71), 0),
        "counts": draw_counts(jax.random.fold_in(splits[4], 71), 0),
        "select": draw_select(jax.random.fold_in(splits[4], 71), 0),
        "cut_weights": draw_cut_weights(jax.random.fold_in(splits[4], 71), 0),
    }


LIMIT = 1048576.0
SCALE = 0.00390625


def square_cell(matrix):
    def step_block(running, block_index):
        left_terms = lax.dynamic_slice_in_dim(matrix, block_index * 32, 32, 1)
        right_terms = lax.dynamic_slice_in_dim(matrix, block_index * 32, 32, 0)
        return jnp.minimum(running, jnp.min(left_terms[:, :, None] + right_terms[None, :, :], axis=1)), None
    initial = jnp.full((CAP, CAP), LIMIT, jnp.float32)
    result, unused = lax.scan(step_block, initial, jnp.arange(CAP // 32, dtype=jnp.int32))
    return result


def reference(weights, counts, select, cut_weights):
    vertex = jnp.arange(CAP, dtype=jnp.int32)
    usable = (vertex[None, :, None] < counts[:, None, None]) & (vertex[None, None, :] < counts[:, None, None])
    matrix = jnp.where(usable, weights, LIMIT)
    matrix = jnp.where((vertex[:, None] == vertex[None, :])[None, :, :], 0.0, matrix).astype(jnp.float32)
    for round_number in range(SQUARINGS):
        matrix = lax.map(square_cell, matrix)

    def pick_block(inputs):
        cell_matrix, chosen = inputs
        return cell_matrix[chosen][:, chosen]

    chosen_blocks = lax.map(pick_block, (matrix, select))

    def parent_block(inputs):
        rows_cut, own_index = inputs
        as_float = rows_cut.astype(jnp.float32).reshape(PB, CELLS, PB)

        def per_child(child_index):
            left_terms = lax.dynamic_index_in_dim(as_float, child_index, 1, keepdims=False)
            right_terms = lax.dynamic_index_in_dim(chosen_blocks, child_index, 0, keepdims=False)
            return jnp.min(left_terms[:, :, None] + right_terms[None, :, :], axis=1)

        child_ids = jnp.arange(CELLS, dtype=jnp.int32)
        best_paths = lax.map(per_child, child_ids)
        own_block = lax.dynamic_index_in_dim(chosen_blocks, own_index, 0, keepdims=False)
        mine = (child_ids == own_index)[:, None, None]
        best_paths = jnp.where(mine, jnp.minimum(best_paths, own_block[None, :, :]), best_paths)
        return jnp.transpose(best_paths, (1, 0, 2)).reshape(PB, CELLS * PB) * SCALE

    return lax.map(parent_block, (cut_weights, jnp.arange(CELLS, dtype=jnp.int32)))
```

```python
import jax
import jax.numpy as jnp
from jax import lax
from jax.experimental import pallas as pl
from jax.experimental.pallas import tpu as pltpu
from jax.sharding import PartitionSpec as P

F32 = jnp.float32
BIG = 1048576.0
SCALE = 0.00390625
NZ, NY, NX = 16, 4, 4
H = 8
CAP = 896
ROWS = 112
PB = 128
SH = 16
L = 16
G = CAP // L
MESH = pl.DeviceIdType.MESH


def slot_cell(h, jj):
    x, c, y, b = h // 2, h % 2, jj // 2, jj % 2
    return (4 * (c + 2 * b) + (x - y) % 4) * NY + y


def lanes(shape):
    return lax.broadcasted_iota(jnp.int32, shape, 1)


def spread(tile, q):
    index = L * q + lanes(tile.shape) % L
    return jnp.take_along_axis(tile, index, axis=1, mode="promise_in_bounds")


def to_rows(block, count):
    turned = jnp.transpose(block)
    lane = lanes((L, PB))
    row = lax.broadcasted_iota(jnp.int32, (L, PB), 0)
    out = []
    for k in range(count):
        part = jnp.zeros((L, PB), F32)
        for q in range(PB // L):
            piece = turned[L * q : L * q + L, :]
            shift = (L * (q - k)) % PB
            if shift:
                piece = pltpu.roll(piece, shift, 1)
            part = jnp.where(lane // L == q, piece, part)
        out.append(jnp.where(lane % L >= row, part, pltpu.roll(part, L, 1)))
    return out


def fold(parts):
    lane = lanes(parts[0].shape)
    d = L // 2
    while d:
        merged = []
        for s in range(d):
            mask = (lane + (2 * PB - s)) % (2 * d) < d
            a = jnp.where(mask, parts[s], parts[s + d])
            b = jnp.where(mask, parts[s + d], parts[s])
            merged.append(jnp.minimum(a, pltpu.roll(b, PB - d, 1)))
        parts = merged
        d //= 2
    return parts[0]


def kernel(
    w_ref, count_ref, sel_ref, selv_ref, cut_ref, o_ref,
    wd, wexp, ablk, abuf, a1, b1r, bnat, a2p, a2r, a2c, a2exp, b2r, piece, cutf, cutr, cutexp, ch, outb,
    s_a, r_a, s_b, r_b, s_p, r_p, s_c, r_c, s_cut, r_cut, s_z, r_z, s_y, r_y, s_o, r_o, l_o,
):
    cell = lax.axis_index("cell")
    me = lax.axis_index("help")
    z, y = cell // NY, cell % NY
    x, core = me // 2, me % 2
    home = 2 * ((z + y) % 4) + (z // 4) % 2
    at_home = home == me
    count = count_ref[0]

    def dev(c, h):
        return {"cell": c, "help": h}

    def peer(r):
        return lax.rem(me + r, H)

    def source_z(b):
        return 4 * (core + 2 * b) + lax.rem(x - y + 4, 4)

    barrier = pltpu.get_barrier_semaphore()

    def greet(c, h):
        pl.semaphore_signal(barrier, inc=1, device_id=dev(c, h), device_id_type=MESH)

    for r in range(1, H):
        greet(cell, peer(r))
    for r in range(1, NY):
        greet(z * NY + lax.rem(y + r, NY), me)
    for b in range(2):
        sz = source_z(b)
        for r in range(H):
            if r:
                greet(sz * NY + y, peer(r))
            else:

                @pl.when(sz != z)
                def _(sz=sz):
                    greet(sz * NY + y, me)

    first = me * ROWS
    shape = (ROWS, PB)
    row = first + lax.broadcasted_iota(jnp.int32, shape, 0)
    tiles = []
    for k in range(CAP // PB):
        t = jnp.where(lanes(shape) + PB * k == row, 0.0, w_ref[0, :, PB * k : PB * k + PB])
        wd[:, PB * k : PB * k + PB] = t
    for h in range(H):
        k, off = (ROWS * h) // PB, (ROWS * h) % PB
        t = wd[:, PB * k : PB * k + PB]
        if off:
            t = pltpu.roll(t, PB - off, 1)
            if off + ROWS > PB:
                n = pltpu.roll(wd[:, PB * k + PB : PB * k + 2 * PB], PB - off, 1)
                t = jnp.where(lanes(shape) < PB - off, t, n)
        ablk[h] = t
    abuf[pl.ds(first, ROWS), :] = ablk[me]
    target = jnp.broadcast_to(selv_ref[...], shape)
    nat = jnp.full(shape, BIG, F32)
    for k in range(CAP // PB):
        got = jnp.take_along_axis(
            wd[:, PB * k : PB * k + PB], target % PB, axis=1, mode="promise_in_bounds"
        )
        nat = jnp.where(target // PB == k, got, nat)
    bnat[0:ROWS, :] = jnp.where(row < count, nat, BIG)
    bnat[ROWS:PB, :] = jnp.full((PB - ROWS, PB), BIG, F32)
    for k, rows in enumerate(to_rows(bnat[...], ROWS // L)):
        b1r[pl.ds(first + L * k, L), :] = rows

    pl.semaphore_wait(barrier, H - 1 + NY - 1 + NZ - jnp.where(at_home, 1, 0))

    def remote(src, dst, ss, rs, c, h):
        return pltpu.make_async_remote_copy(
            src_ref=src, dst_ref=dst, send_sem=ss, recv_sem=rs, device_id=dev(c, h), device_id_type=MESH
        )

    mine = pl.ds(first, ROWS)
    send_a = [
        remote(ablk.at[peer(r)], abuf.at[mine], s_a.at[r], r_a.at[r], cell, peer(r)) for r in range(1, H)
    ]
    for c in send_a:
        c.start()
    send_b = [remote(b1r.at[mine], b1r.at[mine], s_b.at[r], r_b.at[r], cell, peer(r)) for r in range(1, H)]
    for c in send_b:
        c.start()

    for g in range(G):
        k, q = g // 8, g % 8
        wexp[g] = spread(wd[:, PB * k : PB * k + PB], q)
    a_row = me * SH + lax.broadcasted_iota(jnp.int32, (SH, PB), 0)
    for h in range(H):
        for jj in range(8):
            j = slot_cell(h, jj)
            t = cut_ref[0, :, PB * j : PB * j + PB].astype(F32)
            cutf[h, jj] = jnp.where((lanes((SH, PB)) == a_row) & (cell == j), 0.0, t)

    for c in send_a:
        c.wait()

    def pick(i, carry):
        a1[pl.ds(i, 1), :] = abuf[pl.ds(sel_ref[0, i], 1), :]
        return carry

    lax.fori_loop(0, PB, pick, 0)
    col = first + lanes((PB, PB))
    a1[...] = jnp.where(col < count, a1[...], BIG)

    send_p = []
    for i in range(NX):
        chip = lax.rem(x + 1 + i, NX)
        s0 = pl.multiple_of(chip * 2 * SH, 2 * SH)
        left = a1[pl.ds(s0, 2 * SH), :]
        acc = jnp.full((2 * SH, CAP), BIG, F32)
        for w in range(ROWS):
            acc = jnp.minimum(acc, left[:, w : w + 1] + wd[w : w + 1, :])
        a2p[pl.ds(s0, 2 * SH), :] = acc
        for cc in range(2) if i < NX - 1 else (None,):
            dst_core = 1 - core if cc is None else cc
            n = 2 * i + (cc or 0)
            c = remote(
                a2p.at[pl.ds(pl.multiple_of(s0 + SH * dst_core, SH), SH)],
                a2r.at[2 * i + core] if cc is not None else a2r.at[2 * i],
                s_p.at[n],
                r_p.at[2 * i + core] if cc is not None else r_p.at[2 * i],
                cell,
                2 * chip + dst_core,
            )
            c.start()
            send_p.append(c)

    for c in send_b:
        c.wait()

    def contract(expanded, rows, groups):
        def step(g, acc):
            e = expanded(g)
            return tuple(jnp.minimum(acc[s], e + rows(g, s)) for s in range(L))

        return fold(list(lax.fori_loop(0, groups, step, tuple(jnp.full((SH, PB), BIG, F32) for _ in range(L)))))

    def two_arcs(k, carry):
        u0 = pl.multiple_of(k * SH, SH)
        got = contract(lambda g: wexp[g, pl.ds(u0, SH), :], lambda g, s: b1r[pl.ds(g * L + s, 1), :], G)
        u = first + u0 + lax.broadcasted_iota(jnp.int32, (SH, PB), 0)
        bnat[pl.ds(u0, SH), :] = jnp.where(u < count, got, BIG)
        return carry

    lax.fori_loop(0, ROWS // SH, two_arcs, 0)
    for k, rows in enumerate(to_rows(bnat[...], ROWS // L)):
        b2r[pl.ds(first + L * k, L), :] = rows
    send_c = [remote(b2r.at[mine], b2r.at[mine], s_c.at[r], r_c.at[r], cell, peer(r)) for r in range(1, H)]
    for c in send_c:
        c.start()
    send_cut = [
        remote(cutf.at[peer(r)], cutr.at[me], s_cut.at[r], r_cut.at[r], cell, peer(r)) for r in range(1, H)
    ]
    for c in send_cut:
        c.start()
    cutr[me] = cutf[me]

    for n in range(7):
        pltpu.make_async_copy(a2r.at[n], a2r.at[n], r_p.at[n]).wait()
    best = a2p[pl.ds(pl.multiple_of(me * SH, SH), SH), :]
    for n in range(7):
        best = jnp.minimum(best, a2r[n])
    a2c[...] = best
    for g in range(G):
        k, q = g // 8, g % 8
        a2exp[g] = spread(a2c[:, PB * k : PB * k + PB], q)
    for c in send_c:
        c.wait()
    bnat[0:SH, :] = contract(lambda g: a2exp[g], lambda g, s: b2r[pl.ds(g * L + s, 1), :], G)
    piece[...] = to_rows(bnat[...], 1)[0]

    b_own = z // 8
    slot_own = 2 * y + b_own
    mine_ch = ch.at[slot_own, pl.ds(pl.multiple_of(me * L, L), L)]
    send_z = []
    for r in range(NZ):
        c = remote(piece, mine_ch, s_z.at[r], r_z.at[b_own * H + me], lax.rem(z + r, NZ) * NY + y, home)
        if r:
            c.start()
        else:

            @pl.when(home != me)
            def _(c=c):
                c.start()

            @pl.when(home == me)
            def _():
                pltpu.make_async_copy(piece, mine_ch, r_z.at[b_own * H + me]).start()

        send_z.append(c)

    for c in send_cut:
        c.wait()

    def widen(n, carry):
        src, jj = n // 8, n % 8
        t = cutr[src, jj]
        for g in range(8):
            cutexp[src, jj, g] = spread(t, g)
        return carry

    lax.fori_loop(0, 64, widen, 0)

    def near(yy):
        d = lax.rem(z - (4 * core + lax.rem(x - yy + 4, 4)) + NZ, NZ)
        return jnp.where((d <= 4) | (d >= 12), 0, 1)

    def parent(jj):
        def one(src, carry):
            got = contract_few(src)
            outb[jj, src] = got * SCALE
            return carry

        def contract_few(src):
            acc = [jnp.full((SH, PB), BIG, F32) for _ in range(L)]
            for g in range(8):
                e = cutexp[src, jj, g]
                for s in range(L):
                    acc[s] = jnp.minimum(acc[s], e + ch[jj, pl.ds(g * L + s, 1), :])
            return fold(acc)

        lax.fori_loop(0, H, one, 0)
        yy, b = jj // 2, lax.rem(jj, 2)
        j = (4 * (core + 2 * b) + lax.rem(x - yy + 4, 4)) * NY + yy
        where = o_ref.at[:, pl.ds(pl.multiple_of(j * PB, PB), PB)]
        for r in range(1, H):
            remote(outb.at[jj, peer(r)], where, s_o.at[r], r_o.at[r], cell, peer(r)).start()
        pltpu.make_async_copy(outb.at[jj, me], where, l_o).start()

    send_y = []
    b_first = near(y)
    for n in range(2):
        b = b_first if n == 0 else 1 - b_first
        jj = 2 * y + b
        for g in range(H):
            part = ch.at[jj, pl.ds(g * L, L)]
            pltpu.make_async_copy(part, part, r_z.at[b * H + g]).wait()
        for r in range(1, NY):
            c = remote(
                ch.at[jj], ch.at[jj], s_y.at[n * NY + r], r_y.at[n * NY + r],
                z * NY + lax.rem(y + r, NY), me,
            )
            c.start()
            send_y.append(c)
        parent(jj)
    for n in range(2):
        for r in range(1, NY):
            yy = lax.rem(y - r + NY, NY)
            b_src = near(yy)
            jj = 2 * yy + (b_src if n == 0 else 1 - b_src)
            pltpu.make_async_copy(ch.at[jj], ch.at[jj], r_y.at[n * NY + r]).wait()
            parent(jj)

    for c in send_p:
        c.wait_send()
    for r, c in enumerate(send_z):
        if r:
            c.wait_send()
        else:

            @pl.when(home != me)
            def _(c=c):
                c.wait_send()

    for c in send_y:
        c.wait_send()
    for r in range(1, H):
        pltpu.make_async_copy(cutf.at[0], cutf.at[0], s_o.at[r]).wait()
        pltpu.make_async_copy(cutf.at[0], cutf.at[0], r_o.at[r]).wait()
    pltpu.make_async_copy(cutf.at[0], cutf.at[0], l_o).wait()


def per_device(weights, counts, select, cut_weights):
    vmem = pl.BlockSpec(memory_space=pltpu.VMEM)
    smem = pl.BlockSpec(memory_space=pltpu.SMEM)

    def v(*shape):
        return pltpu.VMEM(shape, F32)

    def sem(n):
        return pltpu.SemaphoreType.DMA((n,))

    out = pl.pallas_call(
        kernel,
        out_shape=jax.ShapeDtypeStruct((SH, NZ * NY * PB), F32),
        in_specs=[vmem, smem, smem, vmem, vmem],
        out_specs=pl.BlockSpec(memory_space=pl.ANY),
        scratch_shapes=[
            v(ROWS, CAP),
            v(G, ROWS, PB),
            v(H, ROWS, PB),
            v(CAP, PB),
            v(PB, PB),
            v(CAP, PB),
            v(PB, PB),
            v(PB, CAP),
            v(7, SH, CAP),
            v(SH, CAP),
            v(G, SH, PB),
            v(CAP, PB),
            v(SH, PB),
            v(H, 8, SH, PB),
            v(H, 8, SH, PB),
            v(H, 8, 8, SH, PB),
            v(8, PB, PB),
            v(8, H, SH, PB),
            sem(H), sem(H), sem(H), sem(H), sem(H), sem(H), sem(H), sem(H), sem(H), sem(H),
            sem(NZ), sem(2 * H), sem(2 * NY), sem(2 * NY), sem(H), sem(H), pltpu.SemaphoreType.DMA,
        ],
        compiler_params=pltpu.CompilerParams(
            collective_id=0, has_side_effects=True, vmem_limit_bytes=48 * 1024 * 1024
        ),
    )(weights, counts, select, select, cut_weights)
    return out[None]


def solution(mesh):
    in_specs = (P("cell", "help", None), P("cell"), P("cell", None), P("cell", "help", None))
    return jax.shard_map(
        per_device, mesh=mesh, in_specs=in_specs, out_specs=P("cell", "help", None), check_vma=False
    )
```

```python
import jax
import jax.numpy as jnp
from jax import lax
from jax.experimental import pallas as pl
from jax.experimental.pallas import tpu as pltpu
from jax.sharding import PartitionSpec as P

F32 = jnp.float32
BIG = 1048576.0
SCALE = 0.00390625
NZ, NY, NX = 16, 4, 4
H = 8
CAP = 896
ROWS = 112
PB = 128
SH = 16
L = 16
G = CAP // L
MESH = pl.DeviceIdType.MESH


def slot_cell(h, jj):
    x, c, y, b = h // 2, lax.rem(h, 2), jj // 2, lax.rem(jj, 2)
    return (4 * (c + 2 * b) + lax.rem(x - y + 4, 4)) * NY + y


def lanes(shape):
    return lax.broadcasted_iota(jnp.int32, shape, 1)


def spread(tile, q):
    index = L * q + (lanes(tile.shape) & (L - 1))
    return jnp.take_along_axis(tile, index, axis=1, mode="promise_in_bounds")


def to_rows(block, count):
    turned = jnp.transpose(block)
    lane = lanes((L, PB))
    row = lax.broadcasted_iota(jnp.int32, (L, PB), 0)
    out = []
    for k in range(count):
        part = jnp.zeros((L, PB), F32)
        for q in range(PB // L):
            piece = turned[L * q : L * q + L, :]
            shift = (L * (q - k)) % PB
            if shift:
                piece = pltpu.roll(piece, shift, 1)
            part = jnp.where(lane >> 4 == q, piece, part)
        out.append(jnp.where((lane & (L - 1)) >= row, part, pltpu.roll(part, L, 1)))
    return out


def fold(parts):
    lane = lanes(parts[0].shape)
    d = L // 2
    while d:
        merged = []
        for s in range(d):
            mask = ((lane - s) & d) == 0
            a = jnp.where(mask, parts[s], parts[s + d])
            b = jnp.where(mask, parts[s + d], parts[s])
            merged.append(jnp.minimum(a, pltpu.roll(b, PB - d, 1)))
        parts = merged
        d //= 2
    return parts[0]


def kernel(
    w_ref, count_ref, sel_ref, selv_ref, cut_ref, o_ref,
    wd, wexp, ablk, abuf, a1, b1r, bnat, accb, a2p, a2q, a2r, a2c, a2exp, b2r, piece, cutb, selb, units, cutf, cutr, cutexp,
    ch, outb,
    s_a, r_a, s_b, r_b, s_bf, r_bf, s_q, r_q, s_p, r_p, s_c, r_c, s_cf, r_cf, s_cut, r_cut, s_z, r_z, s_f, r_f, s_y, r_y,
    s_o, r_o, l_o, l_in,
):
    cell = lax.axis_index("cell")
    me = lax.axis_index("help")
    z, y = cell // NY, cell % NY
    x, core = me // 2, me % 2
    home = 2 * ((z + y) % 4) + (z // 4) % 2
    at_home = home == me
    count = count_ref[0]

    def dev(c, h):
        return {"cell": c, "help": h}

    def peer(r):
        return lax.rem(me + r, H)

    def source_z(b):
        return 4 * (core + 2 * b) + lax.rem(x - y + 4, 4)

    loads = [
        pltpu.make_async_copy(w_ref.at[0], wd, l_in.at[0]),
        pltpu.make_async_copy(selv_ref, selb, l_in.at[1]),
        pltpu.make_async_copy(cut_ref.at[0], cutb, l_in.at[2]),
    ]
    for c in loads:
        c.start()

    barrier = pltpu.get_barrier_semaphore()

    def greet(c, h):
        pl.semaphore_signal(barrier, inc=1, device_id=dev(c, h), device_id_type=MESH)

    def along(zz):
        return lax.rem(zz + NZ, NZ)

    def is_near(d):
        return (d <= 4) | (d >= NZ - 4)

    for r in range(1, 5):
        greet(along(z + r) * NY + y, me)
        greet(along(z - r) * NY + y, me)
    for b in range(2):
        sz = source_z(b)

        @pl.when(is_near(along(z - sz)))
        def _(sz=sz):
            for r in range(1, H):
                greet(sz * NY + y, peer(r))

        @pl.when(is_near(along(z - sz)) & (sz != z))
        def _(sz=sz):
            greet(sz * NY + y, me)

    for r in range(1, NY):
        greet(z * NY + lax.rem(y + r, NY), me)
    for r in range(1, H):
        greet(cell, peer(r))

    first = me * ROWS
    shape = (ROWS, PB)
    row = first + lax.broadcasted_iota(jnp.int32, shape, 0)
    loads[0].wait()
    for k in range(CAP // PB):
        t = jnp.where(lanes(shape) + PB * k == row, 0.0, wd[:, PB * k : PB * k + PB])
        wd[:, PB * k : PB * k + PB] = t
    for h in range(H):
        k, off = (ROWS * h) // PB, (ROWS * h) % PB
        t = wd[:, PB * k : PB * k + PB]
        if off:
            t = pltpu.roll(t, PB - off, 1)
            if off + ROWS > PB:
                n = pltpu.roll(wd[:, PB * k + PB : PB * k + 2 * PB], PB - off, 1)
                t = jnp.where(lanes(shape) < PB - off, t, n)
        ablk[h] = t
    abuf[pl.ds(first, ROWS), :] = ablk[me]
    loads[1].wait()
    target = jnp.broadcast_to(selb[...], shape)
    nat = jnp.full(shape, BIG, F32)
    for k in range(CAP // PB):
        got = jnp.take_along_axis(
            wd[:, PB * k : PB * k + PB], target & (PB - 1), axis=1, mode="promise_in_bounds"
        )
        nat = jnp.where(target >> 7 == k, got, nat)
    bnat[0:ROWS, :] = jnp.where(row < count, nat, BIG)
    bnat[ROWS:PB, :] = jnp.full((PB - ROWS, PB), BIG, F32)
    for k, rows in enumerate(to_rows(bnat[...], ROWS // L)):
        b1r[pl.ds(first + L * k, L), :] = rows

    def widen_w(k, carry):
        t = wd[:, pl.ds(pl.multiple_of(k * PB, PB), PB)]
        for q in range(8):
            wexp[8 * k + q] = spread(t, q)
        return carry

    lax.fori_loop(0, CAP // PB, widen_w, 0)
    unit_row = lax.broadcasted_iota(jnp.int32, (PB, PB), 0)
    for g in range(8):
        units[:, PB * g : PB * g + PB] = jnp.where(
            unit_row == L * g + (lanes((PB, PB)) & (L - 1)), 1.0, 0.0
        ).astype(jnp.bfloat16)

    def clear(k, carry):
        accb[k] = jnp.full((L, SH, PB), BIG, F32)
        return carry

    lax.fori_loop(0, ROWS // SH, clear, 0)
    loads[2].wait()

    pl.semaphore_wait(barrier, H - 1 + NY - 1 + 8 + 9 - jnp.where(at_home, 1, 0))

    def remote(src, dst, ss, rs, c, h):
        return pltpu.make_async_remote_copy(
            src_ref=src, dst_ref=dst, send_sem=ss, recv_sem=rs, device_id=dev(c, h), device_id_type=MESH
        )

    mine = pl.ds(first, ROWS)
    partner = 2 * x + 1 - core

    def rows_of(h):
        return pl.ds(pl.multiple_of(h * ROWS, L), ROWS)

    def share(buf, ss, rs, n):
        to = partner if n == 0 else 2 * lax.rem(x + n, NX) + core
        return remote(buf.at[mine], buf.at[mine], ss.at[n], rs.at[n], cell, to)

    def pass_on(buf, ss, rs, n):
        part = buf.at[rows_of(2 * lax.rem(x - n + NX, NX) + core)]
        return remote(part, part, ss.at[n], rs.at[n], cell, partner)

    for n in (1, 3, 2, 0):
        share(b1r, s_b, r_b, n).start()
    send_a = [
        remote(ablk.at[peer(r)], abuf.at[mine], s_a.at[r], r_a.at[r], cell, peer(r)) for r in range(1, H)
    ]
    for c in send_a:
        c.start()

    a_row = me * SH + lax.broadcasted_iota(jnp.int32, (SH, PB), 0)

    def widen_cut(n, carry):
        h, jj = n // 8, lax.rem(n, 8)
        j = slot_cell(h, jj)
        t = cutb[:, pl.ds(pl.multiple_of(j * PB, PB), PB)].astype(F32)
        cutf[h, jj] = jnp.where((lanes((SH, PB)) == a_row) & (cell == j), 0.0, t)
        return carry

    lax.fori_loop(0, 64, widen_cut, 0, unroll=4)

    send_cut = [
        remote(cutf.at[peer(r)], cutr.at[me], s_cut.at[r], r_cut.at[r], cell, peer(r)) for r in range(1, H)
    ]
    for c in send_cut[0:2]:
        c.start()
    cutr[me] = cutf[me]

    def over_block(n, carry):
        m = lax.rem(n + 1, 3)
        hop = jnp.where(n < 2, 0, jnp.where(m == 0, 1, jnp.where(m == 1, 3, 2)))
        same = (n == 0) | ((n >= 2) & (n < 5))
        src = 2 * lax.rem(x - hop + NX, NX) + jnp.where(same, core, 1 - core)

        @pl.when((n >= 1) & (n < 5))
        def _():
            pltpu.make_async_copy(b1r.at[mine], b1r.at[mine], r_b.at[hop]).wait()

        @pl.when((n >= 2) & (n < 5))
        def _():
            pass_on(b1r, s_bf, r_bf, hop).start()

        @pl.when(n >= 5)
        def _():
            pltpu.make_async_copy(b1r.at[mine], b1r.at[mine], r_bf.at[hop]).wait()

        r0 = pl.multiple_of(src * ROWS, L)

        def rows_u(k, carry):
            u0 = pl.multiple_of(k * SH, SH)
            acc = [accb[k, s] for s in range(L)]
            for q in range(ROWS // L):
                e = wexp[src * (ROWS // L) + q, pl.ds(u0, SH), :]
                for s in range(L):
                    acc[s] = jnp.minimum(acc[s], e + b1r[pl.ds(r0 + (q * L + s), 1), :])
            for s in range(L):
                accb[k, s] = acc[s]
            return carry

        lax.fori_loop(0, ROWS // SH, rows_u, 0)
        return carry

    lax.fori_loop(0, H, over_block, 0)

    def finish(k, carry):
        u0 = pl.multiple_of(k * SH, SH)
        u = first + u0 + lax.broadcasted_iota(jnp.int32, (SH, PB), 0)
        bnat[pl.ds(u0, SH), :] = jnp.where(u < count, fold([accb[k, s] for s in range(L)]), BIG)
        return carry

    lax.fori_loop(0, ROWS // SH, finish, 0, unroll=True)
    for k, rows in enumerate(to_rows(bnat[...], ROWS // L)):
        b2r[pl.ds(first + L * k, L), :] = rows
    for n in (1, 3, 2, 0):
        share(b2r, s_c, r_c, n).start()
    for c in send_cut[2:4]:
        c.start()

    for c in send_a:
        c.wait()

    def pick(i, carry):
        a1[pl.ds(i, 1), :] = abuf[pl.ds(sel_ref[0, i], 1), :]
        return carry

    lax.fori_loop(0, PB, pick, 0, unroll=8)
    col = first + lanes((PB, PB))
    a1[...] = jnp.where(col < count, a1[...], BIG)

    def strip(chip, cc):
        return pl.ds(pl.multiple_of((2 * chip + cc) * SH, SH), SH)

    def cross(i, chip):
        return remote(a2p.at[strip(chip, 1 - core)], a2q.at[i], s_q.at[i], r_q.at[i], cell, partner)

    def merged(i):
        chip = lax.rem(x + 1 + i, NX)
        at = strip(chip, core)
        pltpu.make_async_copy(a2q.at[i], a2q.at[i], r_q.at[i]).wait()
        a2p[at, :] = jnp.minimum(a2p[at, :], a2q[i])
        return remote(a2p.at[at], a2r.at[i], s_p.at[i], r_p.at[i], cell, 2 * chip + core)

    def from_chosen(i, carry):
        chip = lax.rem(x + 1 + i, NX)
        s0 = pl.multiple_of(chip * 2 * SH, 2 * SH)
        left = a1[pl.ds(s0, 2 * SH), :]

        acc = jnp.full((2 * SH, CAP), BIG, F32)
        for w in range(ROWS):
            acc = jnp.minimum(acc, left[:, w : w + 1] + wd[w : w + 1, :])
        a2p[pl.ds(s0, 2 * SH), :] = acc
        cross(i, chip).start()

        @pl.when(i >= 1)
        def _():
            merged(i - 1).start()

        return carry

    lax.fori_loop(0, NX, from_chosen, 0)

    for n in (1, 3, 2):
        pltpu.make_async_copy(b2r.at[mine], b2r.at[mine], r_c.at[n]).wait()
        pass_on(b2r, s_cf, r_cf, n).start()
    for c in send_cut[4:]:
        c.start()
    def contract(expanded, rows, groups):
        def step(k, acc):
            acc = list(acc)
            for q in range(8):
                e = expanded(8 * k + q)
                for s in range(L):
                    acc[s] = jnp.minimum(acc[s], e + rows(k * PB, q * L + s))
            return tuple(acc)

        acc = tuple(jnp.full((SH, PB), BIG, F32) for _ in range(L))
        return fold(list(lax.fori_loop(0, groups // 8, step, acc)))

    for n in range(NX - 1):
        pltpu.make_async_copy(a2r.at[n], a2r.at[n], r_p.at[n]).wait()
    pltpu.make_async_copy(a2q.at[NX - 1], a2q.at[NX - 1], r_q.at[NX - 1]).wait()
    best = jnp.minimum(a2p[strip(x, core), :], a2q[NX - 1])
    for n in range(NX - 1):
        best = jnp.minimum(best, a2r[n])
    a2c[...] = best
    for g in range(G):
        k, q = g // 8, g % 8
        a2exp[g] = spread(a2c[:, PB * k : PB * k + PB], q)
    pltpu.make_async_copy(b2r.at[mine], b2r.at[mine], r_c.at[0]).wait()
    for n in (1, 3, 2):
        pltpu.make_async_copy(b2r.at[mine], b2r.at[mine], r_cf.at[n]).wait()
    bnat[0:SH, :] = contract(lambda g: a2exp[g], lambda r0, r: b2r[pl.ds(pl.multiple_of(r0, PB) + r, 1), :], G)
    piece[...] = to_rows(bnat[...], 1)[0]

    b_own = z // 8
    slot_own = 2 * y + b_own
    mine_ch = ch.at[slot_own, pl.ds(pl.multiple_of(me * L, L), L)]

    def to_home(r):
        return remote(piece, mine_ch, s_z.at[r + 4], r_z.at[b_own * H + me], along(z + r) * NY + y, home)

    for r in (4, -4, 3, -3, 2, -2, 1, -1):
        to_home(r).start()

    @pl.when(home != me)
    def _():
        to_home(0).start()

    @pl.when(home == me)
    def _():
        pltpu.make_async_copy(piece, mine_ch, r_z.at[b_own * H + me]).start()

    for c in send_cut:
        c.wait()

    def widen(src, carry):
        t = cutr[src].reshape(PB, PB).astype(jnp.bfloat16)
        wide = jnp.dot(t, units[...], preferred_element_type=F32)
        for g in range(8):
            cutexp[src, g] = wide[:, PB * g : PB * g + PB]
        return carry

    lax.fori_loop(0, H, widen, 0)

    def from_source(yy, b):
        return along(z - (4 * (core + 2 * b) + lax.rem(x - yy + 4, 4)))

    def near(yy):
        return jnp.where(is_near(from_source(yy, 0)), 0, 1)

    def forward(jj, b, r):
        n = b * 8 + r + 3
        return remote(ch.at[jj], ch.at[jj], s_f.at[n], r_f.at[b], along(z + r) * NY + y, me)

    def parent(jj):
        def one(src, carry):
            got = contract_few(src)
            outb[jj, src] = got * SCALE
            return carry

        def contract_few(src):
            acc = [None] * L
            for g in range(8):
                e = cutexp[src, g, pl.ds(pl.multiple_of(jj * SH, SH), SH), :]
                for s in range(L):
                    sums = e + ch[jj, pl.ds(g * L + s, 1), :]
                    acc[s] = jnp.minimum(acc[s], sums) if g else sums
            return fold(acc)

        lax.fori_loop(0, H, one, 0, unroll=4)
        yy, b = jj // 2, lax.rem(jj, 2)
        j = (4 * (core + 2 * b) + lax.rem(x - yy + 4, 4)) * NY + yy
        where = o_ref.at[:, pl.ds(pl.multiple_of(j * PB, PB), PB)]
        for r in range(1, H):
            remote(outb.at[jj, peer(r)], where, s_o.at[r], r_o.at[r], cell, peer(r)).start()
        pltpu.make_async_copy(outb.at[jj, me], where, l_o).start()

    def along_y(r, jj, which):
        sem = which * NY + r
        return remote(ch.at[jj], ch.at[jj], s_y.at[sem], r_y.at[sem], z * NY + lax.rem(y + r, NY), me)

    def take(b, which):
        jj = 2 * y + b
        d = from_source(y, b)

        @pl.when(is_near(d))
        def _():
            for g in range(H):
                part = ch.at[jj, pl.ds(g * L, L)]
                pltpu.make_async_copy(part, part, r_z.at[b * H + g]).wait()

        @pl.when(jnp.logical_not(is_near(d)))
        def _():
            pltpu.make_async_copy(ch.at[jj], ch.at[jj], r_f.at[b]).wait()

        @pl.when(d == 4)
        def _():
            for k in (4, 3, 2, 1):
                forward(jj, b, k).start()

        @pl.when(d == NZ - 4)
        def _():
            for k in (3, 2, 1):
                forward(jj, b, -k).start()

        for k in range(1, NY):
            along_y(k, jj, which).start()

    b_near = near(y)
    both_near = is_near(from_source(y, 1 - b_near))

    def serve(n, carry):
        which, r = n // NY, lax.rem(n, NY)
        yy = lax.rem(y - r + NY, NY)
        first_b = near(yy)
        b = jnp.where(which == 0, first_b, 1 - first_b)
        jj = 2 * yy + b

        @pl.when(n == 0)
        def _():
            take(b_near, 0)

        @pl.when(((n == 0) & both_near) | ((n == NY) & jnp.logical_not(both_near)))
        def _():
            take(1 - b_near, 1)

        @pl.when(r > 0)
        def _():
            pltpu.make_async_copy(ch.at[jj], ch.at[jj], r_y.at[which * NY + r]).wait()

        parent(jj)
        return carry

    lax.fori_loop(0, 8, serve, 0)

    for n in range(NX):
        pltpu.make_async_copy(a2q.at[0], a2q.at[0], s_q.at[n]).wait()
        if n < NX - 1:
            pltpu.make_async_copy(a2q.at[0], a2q.at[0], s_p.at[n]).wait()
    for n in range(NX):
        share(b1r, s_b, r_b, n).wait_send()
        share(b2r, s_c, r_c, n).wait_send()
        if n:
            pass_on(b1r, s_bf, r_bf, n).wait_send()
            pass_on(b2r, s_cf, r_cf, n).wait_send()
    for r in range(-4, 5):
        if r:
            to_home(r).wait_send()

    @pl.when(home != me)
    def _():
        to_home(0).wait_send()

    for b in range(2):
        d = from_source(y, b)

        @pl.when(d == 4)
        def _(b=b):
            for k in range(1, 5):
                forward(2 * y + b, b, k).wait_send()

        @pl.when(d == NZ - 4)
        def _(b=b):
            for k in range(1, 4):
                forward(2 * y + b, b, -k).wait_send()

    for which in range(2):
        for r in range(1, NY):
            along_y(r, 2 * y, which).wait_send()
    for r in range(1, H):
        pltpu.make_async_copy(cutf.at[0], cutf.at[0], s_o.at[r]).wait()
        pltpu.make_async_copy(cutf.at[0], cutf.at[0], r_o.at[r]).wait()
    pltpu.make_async_copy(cutf.at[0], cutf.at[0], l_o).wait()


def per_device(weights, counts, select, cut_weights):
    hbm = pl.BlockSpec(memory_space=pltpu.HBM)
    smem = pl.BlockSpec(memory_space=pltpu.SMEM)

    def hold(a):
        return pltpu.with_memory_space_constraint(a, pltpu.HBM)

    def v(*shape):
        return pltpu.VMEM(shape, F32)

    def sem(n):
        return pltpu.SemaphoreType.DMA((n,))

    out = pl.pallas_call(
        kernel,
        out_shape=jax.ShapeDtypeStruct((SH, NZ * NY * PB), F32),
        in_specs=[hbm, smem, smem, hbm, hbm],
        out_specs=hbm,
        scratch_shapes=[
            v(ROWS, CAP),
            v(G, ROWS, PB),
            v(H, ROWS, PB),
            v(CAP, PB),
            v(PB, PB),
            v(CAP, PB),
            v(PB, PB),
            v(ROWS // SH, L, SH, PB),
            v(PB, CAP),
            v(NX, SH, CAP),
            v(NX - 1, SH, CAP),
            v(SH, CAP),
            v(G, SH, PB),
            v(CAP, PB),
            v(SH, PB),
            pltpu.VMEM((SH, NZ * NY * PB), jnp.bfloat16),
            pltpu.VMEM((1, PB), jnp.int32),
            pltpu.VMEM((PB, 8 * PB), jnp.bfloat16),
            v(H, 8, SH, PB),
            v(H, 8, SH, PB),
            v(H, 8, PB, PB),
            v(8, PB, PB),
            v(8, H, SH, PB),
            sem(H), sem(H), sem(NX), sem(NX), sem(NX), sem(NX), sem(NX), sem(NX), sem(NX), sem(NX), sem(NX), sem(NX), sem(NX), sem(NX),
            sem(H), sem(H), sem(9), sem(2 * H), sem(16), sem(2), sem(2 * NY), sem(2 * NY), sem(H), sem(H),
            pltpu.SemaphoreType.DMA, sem(3),
        ],
        compiler_params=pltpu.CompilerParams(
            collective_id=0, has_side_effects=True, vmem_limit_bytes=48 * 1024 * 1024
        ),
    )(hold(weights), counts, select, hold(select), hold(cut_weights))
    return out[None]


def solution(mesh):
    in_specs = (P("cell", "help", None), P("cell"), P("cell", None), P("cell", "help", None))
    return jax.shard_map(
        per_device, mesh=mesh, in_specs=in_specs, out_specs=P("cell", "help", None), check_vma=False
    )
```

```python
import jax
import jax.numpy as jnp
from jax import lax
from jax.experimental import pallas as pl
from jax.experimental.pallas import tpu as pltpu
from jax.sharding import PartitionSpec as P

F32 = jnp.float32
BIG = 1048576.0
SCALE = 0.00390625
NZ, NY, NX = 16, 4, 4
H = 8
CAP = 896
ROWS = 112
PB = 128
SH = 16
L = 16
G = CAP // L
MESH = pl.DeviceIdType.MESH


def slot_cell(h, jj):
    x, c, y, b = h // 2, lax.rem(h, 2), jj // 2, lax.rem(jj, 2)
    return (4 * (c + 2 * b) + lax.rem(x - y + 4, 4)) * NY + y


def lanes(shape):
    return lax.broadcasted_iota(jnp.int32, shape, 1)


def spread(tile, q):
    index = L * q + (lanes(tile.shape) & (L - 1))
    return jnp.take_along_axis(tile, index, axis=1, mode="promise_in_bounds")


def to_rows(block, count):
    turned = jnp.transpose(block)
    lane = lanes((L, PB))
    row = lax.broadcasted_iota(jnp.int32, (L, PB), 0)
    out = []
    for k in range(count):
        part = jnp.zeros((L, PB), F32)
        for q in range(PB // L):
            piece = turned[L * q : L * q + L, :]
            shift = (L * (q - k)) % PB
            if shift:
                piece = pltpu.roll(piece, shift, 1)
            part = jnp.where(lane >> 4 == q, piece, part)
        out.append(jnp.where((lane & (L - 1)) >= row, part, pltpu.roll(part, L, 1)))
    return out


def fold(parts):
    lane = lanes(parts[0].shape)
    d = L // 2
    while d:
        merged = []
        for s in range(d):
            mask = ((lane - s) & d) == 0
            a = jnp.where(mask, parts[s], parts[s + d])
            b = jnp.where(mask, parts[s + d], parts[s])
            merged.append(jnp.minimum(a, pltpu.roll(b, PB - d, 1)))
        parts = merged
        d //= 2
    return parts[0]


def kernel(
    w_ref, count_ref, sel_ref, selv_ref, cut_ref, o_ref,
    wd, wexp, ablk, abuf, a1, b1r, bnat, accb, a2p, a2q, a2r, a2c, a2exp, b2r, piece, cutb, selb, sels, units, cutf, cutr, cutexp,
    ch, outb,
    s_a, r_a, s_b, r_b, s_bf, r_bf, s_q, r_q, s_p, r_p, s_c, r_c, s_cf, r_cf, s_cut, r_cut, s_z, r_z, s_f, r_f, s_y, r_y,
    s_o, r_o, l_o, l_in,
):
    cell = lax.axis_index("cell")
    me = lax.axis_index("help")
    z, y = cell // NY, cell % NY
    x, core = me // 2, me % 2
    home = 2 * ((z + y) % 4) + (z // 4) % 2
    at_home = home == me

    def dev(c, h):
        return {"cell": c, "help": h}

    def peer(r):
        return lax.rem(me + r, H)

    def source_z(b):
        return 4 * (core + 2 * b) + lax.rem(x - y + 4, 4)

    loads = [
        pltpu.make_async_copy(w_ref.at[0], wd, l_in.at[0]),
        pltpu.make_async_copy(selv_ref, selb, l_in.at[1]),
        pltpu.make_async_copy(cut_ref.at[0], cutb, l_in.at[2]),
        pltpu.make_async_copy(sel_ref, sels, l_in.at[3]),
    ]
    for c in loads:
        c.start()

    barrier = pltpu.get_barrier_semaphore()

    def greet(c, h):
        pl.semaphore_signal(barrier, inc=1, device_id=dev(c, h), device_id_type=MESH)

    def along(zz):
        return lax.rem(zz + NZ, NZ)

    def is_near(d):
        return (d <= 4) | (d >= NZ - 4)

    for b in range(2):
        sz = source_z(b)

        @pl.when(is_near(along(z - sz)))
        def _(sz=sz):
            for r in range(1, H):
                greet(sz * NY + y, peer(r))

        @pl.when(is_near(along(z - sz)) & (sz != z))
        def _(sz=sz):
            greet(sz * NY + y, me)

    for r in (4, 3, 2, 1):
        greet(along(z + r) * NY + y, me)
        greet(along(z - r) * NY + y, me)
    for r in range(1, NY):
        greet(z * NY + lax.rem(y + r, NY), me)
    for r in range(1, H):
        greet(cell, peer(r))

    first = me * ROWS
    shape = (ROWS, PB)
    row = first + lax.broadcasted_iota(jnp.int32, shape, 0)
    loads[0].wait()
    for k in range(CAP // PB):
        t = jnp.where(lanes(shape) + PB * k == row, 0.0, wd[:, PB * k : PB * k + PB])
        wd[:, PB * k : PB * k + PB] = t
    for h in range(H):
        k, off = (ROWS * h) // PB, (ROWS * h) % PB
        t = wd[:, PB * k : PB * k + PB]
        if off:
            t = pltpu.roll(t, PB - off, 1)
            if off + ROWS > PB:
                n = pltpu.roll(wd[:, PB * k + PB : PB * k + 2 * PB], PB - off, 1)
                t = jnp.where(lanes(shape) < PB - off, t, n)
        ablk[h] = t
    abuf[pl.ds(first, ROWS), :] = ablk[me]
    loads[1].wait()
    loads[3].wait()
    count = count_ref[0]
    target = jnp.broadcast_to(selb[...], shape)
    nat = jnp.full(shape, BIG, F32)
    for k in range(CAP // PB):
        got = jnp.take_along_axis(
            wd[:, PB * k : PB * k + PB], target & (PB - 1), axis=1, mode="promise_in_bounds"
        )
        nat = jnp.where(target >> 7 == k, got, nat)
    bnat[0:ROWS, :] = jnp.where(row < count, nat, BIG)
    bnat[ROWS:PB, :] = jnp.full((PB - ROWS, PB), BIG, F32)
    for k, rows in enumerate(to_rows(bnat[...], ROWS // L)):
        b1r[pl.ds(first + L * k, L), :] = rows

    def widen_w(k, carry):
        t = wd[:, pl.ds(pl.multiple_of(k * PB, PB), PB)]
        for q in range(8):
            wexp[8 * k + q] = spread(t, q)
        return carry

    lax.fori_loop(0, CAP // PB, widen_w, 0)
    unit_row = lax.broadcasted_iota(jnp.int32, (PB, PB), 0)
    for g in range(8):
        units[:, PB * g : PB * g + PB] = jnp.where(
            unit_row == L * g + (lanes((PB, PB)) & (L - 1)), 1.0, 0.0
        ).astype(jnp.bfloat16)

    def clear(k, carry):
        accb[k] = jnp.full((L, SH, PB), BIG, F32)
        return carry

    lax.fori_loop(0, ROWS // SH, clear, 0)
    loads[2].wait()

    pl.semaphore_wait(barrier, H - 1 + NY - 1 + 8 + 9 - jnp.where(at_home, 1, 0))

    def remote(src, dst, ss, rs, c, h):
        return pltpu.make_async_remote_copy(
            src_ref=src, dst_ref=dst, send_sem=ss, recv_sem=rs, device_id=dev(c, h), device_id_type=MESH
        )

    mine = pl.ds(first, ROWS)
    partner = 2 * x + 1 - core

    def rows_of(h):
        return pl.ds(pl.multiple_of(h * ROWS, L), ROWS)

    def share(buf, ss, rs, n):
        to = partner if n == 0 else 2 * lax.rem(x + n, NX) + core
        return remote(buf.at[mine], buf.at[mine], ss.at[n], rs.at[n], cell, to)

    def pass_on(buf, ss, rs, n):
        part = buf.at[rows_of(2 * lax.rem(x - n + NX, NX) + core)]
        return remote(part, part, ss.at[n], rs.at[n], cell, partner)

    for n in (0, 1, 3, 2):
        share(b1r, s_b, r_b, n).start()
    send_a = [
        remote(ablk.at[peer(r)], abuf.at[mine], s_a.at[r], r_a.at[r], cell, peer(r)) for r in range(1, H)
    ]
    for c in send_a:
        c.start()

    a_row = me * SH + lax.broadcasted_iota(jnp.int32, (SH, PB), 0)

    def widen_cut(n, carry):
        h, jj = n // 8, lax.rem(n, 8)
        j = slot_cell(h, jj)
        t = cutb[:, pl.ds(pl.multiple_of(j * PB, PB), PB)].astype(F32)
        cutf[h, jj] = jnp.where((lanes((SH, PB)) == a_row) & (cell == j), 0.0, t)
        return carry

    lax.fori_loop(0, 64, widen_cut, 0, unroll=4)

    send_cut = [
        remote(cutf.at[peer(r)], cutr.at[me], s_cut.at[r], r_cut.at[r], cell, peer(r)) for r in range(1, H)
    ]
    for c in send_cut[0:4]:
        c.start()
    cutr[me] = cutf[me]

    def over_block(n, carry):
        m = lax.rem(n + 1, 3)
        hop = jnp.where(n < 2, 0, jnp.where(m == 0, 1, jnp.where(m == 1, 3, 2)))
        same = (n == 0) | ((n >= 2) & (n < 5))
        src = 2 * lax.rem(x - hop + NX, NX) + jnp.where(same, core, 1 - core)

        @pl.when((n >= 1) & (n < 5))
        def _():
            pltpu.make_async_copy(b1r.at[mine], b1r.at[mine], r_b.at[hop]).wait()

        @pl.when((n >= 2) & (n < 5))
        def _():
            pass_on(b1r, s_bf, r_bf, hop).start()

        @pl.when(n >= 5)
        def _():
            pltpu.make_async_copy(b1r.at[mine], b1r.at[mine], r_bf.at[hop]).wait()

        r0 = pl.multiple_of(src * ROWS, L)

        def rows_u(k, carry):
            u0 = pl.multiple_of(k * SH, SH)
            acc = [accb[k, s] for s in range(L)]
            for q in range(ROWS // L):
                e = wexp[src * (ROWS // L) + q, pl.ds(u0, SH), :]
                for s in range(L):
                    acc[s] = jnp.minimum(acc[s], e + b1r[pl.ds(r0 + (q * L + s), 1), :])
            for s in range(L):
                accb[k, s] = acc[s]
            return carry

        lax.fori_loop(0, ROWS // SH, rows_u, 0)
        return carry

    lax.fori_loop(0, H, over_block, 0)

    def finish(k, carry):
        u0 = pl.multiple_of(k * SH, SH)
        u = first + u0 + lax.broadcasted_iota(jnp.int32, (SH, PB), 0)
        bnat[pl.ds(u0, SH), :] = jnp.where(u < count, fold([accb[k, s] for s in range(L)]), BIG)
        return carry

    lax.fori_loop(0, ROWS // SH, finish, 0, unroll=True)
    for k, rows in enumerate(to_rows(bnat[...], ROWS // L)):
        b2r[pl.ds(first + L * k, L), :] = rows
    for n in (1, 3, 2, 0):
        share(b2r, s_c, r_c, n).start()
    for c in send_cut[4:]:
        c.start()

    for c in send_a:
        c.wait()

    def pick(i, carry):
        a1[pl.ds(i, 1), :] = abuf[pl.ds(sels[0, i], 1), :]
        return carry

    lax.fori_loop(0, PB, pick, 0, unroll=8)
    col = first + lanes((PB, PB))
    a1[...] = jnp.where(col < count, a1[...], BIG)

    def strip(chip, cc):
        return pl.ds(pl.multiple_of((2 * chip + cc) * SH, SH), SH)

    def cross(i, chip):
        return remote(a2p.at[strip(chip, 1 - core)], a2q.at[i], s_q.at[i], r_q.at[i], cell, partner)

    def merged(i):
        chip = lax.rem(x + 1 + i, NX)
        at = strip(chip, core)
        pltpu.make_async_copy(a2q.at[i], a2q.at[i], r_q.at[i]).wait()
        a2p[at, :] = jnp.minimum(a2p[at, :], a2q[i])
        return remote(a2p.at[at], a2r.at[i], s_p.at[i], r_p.at[i], cell, 2 * chip + core)

    def from_chosen(i, carry):
        chip = lax.rem(x + 1 + i, NX)
        s0 = pl.multiple_of(chip * 2 * SH, 2 * SH)
        left = a1[pl.ds(s0, 2 * SH), :]

        acc = jnp.full((2 * SH, CAP), BIG, F32)
        for w in range(ROWS):
            acc = jnp.minimum(acc, left[:, w : w + 1] + wd[w : w + 1, :])
        a2p[pl.ds(s0, 2 * SH), :] = acc
        cross(i, chip).start()

        @pl.when(i >= 1)
        def _():
            merged(i - 1).start()

        return carry

    lax.fori_loop(0, NX, from_chosen, 0)

    for n in (1, 3, 2):
        pltpu.make_async_copy(b2r.at[mine], b2r.at[mine], r_c.at[n]).wait()
        pass_on(b2r, s_cf, r_cf, n).start()
    def contract(expanded, rows, groups):
        def step(k, acc):
            acc = list(acc)
            for q in range(8):
                e = expanded(8 * k + q)
                for s in range(L):
                    acc[s] = jnp.minimum(acc[s], e + rows(k * PB, q * L + s))
            return tuple(acc)

        acc = tuple(jnp.full((SH, PB), BIG, F32) for _ in range(L))
        return fold(list(lax.fori_loop(0, groups // 8, step, acc)))

    for n in range(NX - 1):
        pltpu.make_async_copy(a2r.at[n], a2r.at[n], r_p.at[n]).wait()
    pltpu.make_async_copy(a2q.at[NX - 1], a2q.at[NX - 1], r_q.at[NX - 1]).wait()
    best = jnp.minimum(a2p[strip(x, core), :], a2q[NX - 1])
    for n in range(NX - 1):
        best = jnp.minimum(best, a2r[n])
    a2c[...] = best
    for g in range(G):
        k, q = g // 8, g % 8
        a2exp[g] = spread(a2c[:, PB * k : PB * k + PB], q)
    pltpu.make_async_copy(b2r.at[mine], b2r.at[mine], r_c.at[0]).wait()
    for n in (1, 3, 2):
        pltpu.make_async_copy(b2r.at[mine], b2r.at[mine], r_cf.at[n]).wait()
    bnat[0:SH, :] = contract(lambda g: a2exp[g], lambda r0, r: b2r[pl.ds(pl.multiple_of(r0, PB) + r, 1), :], G)
    piece[...] = to_rows(bnat[...], 1)[0]

    b_own = z // 8
    slot_own = 2 * y + b_own
    mine_ch = ch.at[slot_own, pl.ds(pl.multiple_of(me * L, L), L)]

    def to_home(r):
        return remote(piece, mine_ch, s_z.at[r + 4], r_z.at[b_own * H + me], along(z + r) * NY + y, home)

    for r in (4, -4, 3, -3, 2, -2, 1, -1):
        to_home(r).start()

    @pl.when(home != me)
    def _():
        to_home(0).start()

    @pl.when(home == me)
    def _():
        pltpu.make_async_copy(piece, mine_ch, r_z.at[b_own * H + me]).start()

    for c in send_cut:
        c.wait()

    def widen(src, carry):
        t = cutr[src].reshape(PB, PB).astype(jnp.bfloat16)
        wide = jnp.dot(t, units[...], preferred_element_type=F32)
        for g in range(8):
            cutexp[src, g] = wide[:, PB * g : PB * g + PB]
        return carry

    lax.fori_loop(0, H, widen, 0)

    def from_source(yy, b):
        return along(z - (4 * (core + 2 * b) + lax.rem(x - yy + 4, 4)))

    def near(yy):
        return jnp.where(is_near(from_source(yy, 0)), 0, 1)

    def forward(jj, b, r):
        n = b * 8 + r + 3
        return remote(ch.at[jj], ch.at[jj], s_f.at[n], r_f.at[b], along(z + r) * NY + y, me)

    def parent(jj):
        def one(src, carry):
            got = contract_few(src)
            outb[jj, src] = got * SCALE
            return carry

        def contract_few(src):
            acc = [None] * L
            for g in range(8):
                e = cutexp[src, g, pl.ds(pl.multiple_of(jj * SH, SH), SH), :]
                for s in range(L):
                    sums = e + ch[jj, pl.ds(g * L + s, 1), :]
                    acc[s] = jnp.minimum(acc[s], sums) if g else sums
            return fold(acc)

        lax.fori_loop(0, H, one, 0, unroll=4)
        yy, b = jj // 2, lax.rem(jj, 2)
        j = (4 * (core + 2 * b) + lax.rem(x - yy + 4, 4)) * NY + yy
        where = o_ref.at[:, pl.ds(pl.multiple_of(j * PB, PB), PB)]
        for r in range(1, H):
            remote(outb.at[jj, peer(r)], where, s_o.at[r], r_o.at[r], cell, peer(r)).start()
        pltpu.make_async_copy(outb.at[jj, me], where, l_o).start()

    def along_y(r, jj, which):
        sem = which * NY + r
        return remote(ch.at[jj], ch.at[jj], s_y.at[sem], r_y.at[sem], z * NY + lax.rem(y + r, NY), me)

    def take(b, which):
        jj = 2 * y + b
        d = from_source(y, b)

        @pl.when(is_near(d))
        def _():
            for g in range(H):
                part = ch.at[jj, pl.ds(g * L, L)]
                pltpu.make_async_copy(part, part, r_z.at[b * H + g]).wait()

        @pl.when(jnp.logical_not(is_near(d)))
        def _():
            pltpu.make_async_copy(ch.at[jj], ch.at[jj], r_f.at[b]).wait()

        @pl.when(d == 4)
        def _():
            for k in (4, 3, 2, 1):
                forward(jj, b, k).start()

        @pl.when(d == NZ - 4)
        def _():
            for k in (3, 2, 1):
                forward(jj, b, -k).start()

        for k in (1, 3, 2):
            along_y(k, jj, which).start()

    b_near = near(y)
    both_near = is_near(from_source(y, 1 - b_near))

    def serve(n, carry):
        which, m = n // NY, lax.rem(n, NY)
        r = jnp.where(m >= 2, 5 - m, m)
        yy = lax.rem(y - r + NY, NY)
        first_b = near(yy)
        b = jnp.where(which == 0, first_b, 1 - first_b)
        jj = 2 * yy + b

        @pl.when(n == 0)
        def _():
            take(b_near, 0)

        @pl.when(((n == 0) & both_near) | ((n == NY) & jnp.logical_not(both_near)))
        def _():
            take(1 - b_near, 1)

        @pl.when(r > 0)
        def _():
            pltpu.make_async_copy(ch.at[jj], ch.at[jj], r_y.at[which * NY + r]).wait()

        parent(jj)
        return carry

    lax.fori_loop(0, 8, serve, 0)

    for n in range(NX):
        pltpu.make_async_copy(a2q.at[0], a2q.at[0], s_q.at[n]).wait()
        if n < NX - 1:
            pltpu.make_async_copy(a2q.at[0], a2q.at[0], s_p.at[n]).wait()
    for n in range(NX):
        share(b1r, s_b, r_b, n).wait_send()
        share(b2r, s_c, r_c, n).wait_send()
        if n:
            pass_on(b1r, s_bf, r_bf, n).wait_send()
            pass_on(b2r, s_cf, r_cf, n).wait_send()
    for r in range(-4, 5):
        if r:
            to_home(r).wait_send()

    @pl.when(home != me)
    def _():
        to_home(0).wait_send()

    for b in range(2):
        d = from_source(y, b)

        @pl.when(d == 4)
        def _(b=b):
            for k in range(1, 5):
                forward(2 * y + b, b, k).wait_send()

        @pl.when(d == NZ - 4)
        def _(b=b):
            for k in range(1, 4):
                forward(2 * y + b, b, -k).wait_send()

    for which in range(2):
        for r in range(1, NY):
            along_y(r, 2 * y, which).wait_send()
    for r in range(1, H):
        pltpu.make_async_copy(cutf.at[0], cutf.at[0], s_o.at[r]).wait()
        pltpu.make_async_copy(cutf.at[0], cutf.at[0], r_o.at[r]).wait()
    pltpu.make_async_copy(cutf.at[0], cutf.at[0], l_o).wait()


def per_device(weights, counts, select, cut_weights):
    hbm = pl.BlockSpec(memory_space=pltpu.HBM)

    def hold(a):
        return pltpu.with_memory_space_constraint(a, pltpu.HBM)

    def v(*shape):
        return pltpu.VMEM(shape, F32)

    def sem(n):
        return pltpu.SemaphoreType.DMA((n,))

    out = pl.pallas_call(
        kernel,
        out_shape=jax.ShapeDtypeStruct((SH, NZ * NY * PB), F32),
        in_specs=[hbm, pl.BlockSpec(memory_space=pltpu.SMEM), hbm, hbm, hbm],
        out_specs=hbm,
        scratch_shapes=[
            v(ROWS, CAP),
            v(G, ROWS, PB),
            v(H, ROWS, PB),
            v(CAP, PB),
            v(PB, PB),
            v(CAP, PB),
            v(PB, PB),
            v(ROWS // SH, L, SH, PB),
            v(PB, CAP),
            v(NX, SH, CAP),
            v(NX - 1, SH, CAP),
            v(SH, CAP),
            v(G, SH, PB),
            v(CAP, PB),
            v(SH, PB),
            pltpu.VMEM((SH, NZ * NY * PB), jnp.bfloat16),
            pltpu.VMEM((1, PB), jnp.int32),
            pltpu.SMEM((1, PB), jnp.int32),
            pltpu.VMEM((PB, 8 * PB), jnp.bfloat16),
            v(H, 8, SH, PB),
            v(H, 8, SH, PB),
            v(H, 8, PB, PB),
            v(8, PB, PB),
            v(8, H, SH, PB),
            sem(H), sem(H), sem(NX), sem(NX), sem(NX), sem(NX), sem(NX), sem(NX), sem(NX), sem(NX), sem(NX), sem(NX), sem(NX), sem(NX),
            sem(H), sem(H), sem(9), sem(2 * H), sem(16), sem(2), sem(2 * NY), sem(2 * NY), sem(H), sem(H),
            pltpu.SemaphoreType.DMA, sem(4),
        ],
        compiler_params=pltpu.CompilerParams(
            collective_id=0, has_side_effects=True, vmem_limit_bytes=48 * 1024 * 1024
        ),
    )(hold(weights), counts, hold(select), hold(select), hold(cut_weights))
    return out[None]


def solution(mesh):
    in_specs = (P("cell", "help", None), P("cell"), P("cell", None), P("cell", "help", None))
    return jax.shard_map(
        per_device, mesh=mesh, in_specs=in_specs, out_specs=P("cell", "help", None), check_vma=False
    )
```

```python
import jax
import jax.numpy as jnp
from jax import lax
from jax.experimental import pallas as pl
from jax.experimental.pallas import tpu as pltpu
from jax.sharding import PartitionSpec as P

F32 = jnp.float32
BIG = 1048576.0
SCALE = 0.00390625
NZ, NY, NX = 16, 4, 4
H = 8
CAP = 896
ROWS = 112
PB = 128
SH = 16
L = 16
G = CAP // L
MESH = pl.DeviceIdType.MESH


def slot_cell(h, jj):
    x, c, y, b = h // 2, lax.rem(h, 2), jj // 2, lax.rem(jj, 2)
    return (4 * (c + 2 * b) + lax.rem(x - y + 4, 4)) * NY + y


def lanes(shape):
    return lax.broadcasted_iota(jnp.int32, shape, 1)


def spread(tile, q):
    index = L * q + (lanes(tile.shape) & (L - 1))
    return jnp.take_along_axis(tile, index, axis=1, mode="promise_in_bounds")


def to_rows(block, count):
    turned = jnp.transpose(block)
    lane = lanes((L, PB))
    row = lax.broadcasted_iota(jnp.int32, (L, PB), 0)
    out = []
    for k in range(count):
        part = jnp.zeros((L, PB), F32)
        for q in range(PB // L):
            piece = turned[L * q : L * q + L, :]
            shift = (L * (q - k)) % PB
            if shift:
                piece = pltpu.roll(piece, shift, 1)
            part = jnp.where(lane >> 4 == q, piece, part)
        out.append(jnp.where((lane & (L - 1)) >= row, part, pltpu.roll(part, L, 1)))
    return out


def fold(parts):
    lane = lanes(parts[0].shape)
    d = L // 2
    while d:
        merged = []
        for s in range(d):
            mask = ((lane - s) & d) == 0
            a = jnp.where(mask, parts[s], parts[s + d])
            b = jnp.where(mask, parts[s + d], parts[s])
            merged.append(jnp.minimum(a, pltpu.roll(b, PB - d, 1)))
        parts = merged
        d //= 2
    return parts[0]


def kernel(
    w_ref, count_ref, selv_ref, cut_ref, o_ref,
    wd, wexp, zs, zq, za, a1, b1r, bnat, accb, a2p, a2q, a2r, a2c, a2exp, b2r, piece, cutb, selb, units, cutf, cutr, cutexp,
    ch, outb,
    s_zq, r_zq, s_a, r_a, s_b, r_b, s_bf, r_bf, s_q, r_q, s_p, r_p, s_c, r_c, s_cf, r_cf, s_cut, r_cut, s_z, r_z, s_f, r_f, s_y, r_y,
    s_o, r_o, l_o, l_in,
):
    cell = lax.axis_index("cell")
    me = lax.axis_index("help")
    z, y = cell // NY, cell % NY
    x, core = me // 2, me % 2
    home = 2 * ((z + y) % 4) + (z // 4) % 2
    at_home = home == me

    def dev(c, h):
        return {"cell": c, "help": h}

    def peer(r):
        return lax.rem(me + r, H)

    def source_z(b):
        return 4 * (core + 2 * b) + lax.rem(x - y + 4, 4)

    loads = [
        pltpu.make_async_copy(w_ref.at[0], wd, l_in.at[0]),
        pltpu.make_async_copy(selv_ref, selb, l_in.at[1]),
        pltpu.make_async_copy(cut_ref.at[0], cutb, l_in.at[2]),
    ]
    for c in loads:
        c.start()

    barrier = pltpu.get_barrier_semaphore()

    def greet(c, h):
        pl.semaphore_signal(barrier, inc=1, device_id=dev(c, h), device_id_type=MESH)

    def along(zz):
        return lax.rem(zz + NZ, NZ)

    def is_near(d):
        return (d <= 4) | (d >= NZ - 4)

    for b in range(2):
        sz = source_z(b)

        @pl.when(is_near(along(z - sz)))
        def _(sz=sz):
            for r in range(1, H):
                greet(sz * NY + y, peer(r))

        @pl.when(is_near(along(z - sz)) & (sz != z))
        def _(sz=sz):
            greet(sz * NY + y, me)

    for r in (4, 3, 2, 1):
        greet(along(z + r) * NY + y, me)
        greet(along(z - r) * NY + y, me)
    for r in range(1, NY):
        greet(z * NY + lax.rem(y + r, NY), me)
    for r in range(1, H):
        greet(cell, peer(r))

    first = me * ROWS
    shape = (ROWS, PB)
    row = first + lax.broadcasted_iota(jnp.int32, shape, 0)
    loads[0].wait()
    for k in range(CAP // PB):
        t = jnp.where(lanes(shape) + PB * k == row, 0.0, wd[:, PB * k : PB * k + PB])
        wd[:, PB * k : PB * k + PB] = t
    loads[1].wait()
    count = count_ref[0]
    spot = lax.broadcasted_iota(jnp.int32, (PB, PB), 0)
    held = (jnp.broadcast_to(selb[...], (PB, PB)) == first + spot) & (spot < ROWS)
    one = jnp.transpose(jnp.where(held, 1.0, 0.0))
    owned = jnp.max(one, axis=1, keepdims=True) > 0.5
    one = one[:, 0:ROWS].astype(jnp.bfloat16)
    for h in range(H):
        k, off = (ROWS * h) // PB, (ROWS * h) % PB
        t = wd[:, PB * k : PB * k + PB]
        if off:
            t = pltpu.roll(t, PB - off, 1)
            if off + ROWS > PB:
                n = pltpu.roll(wd[:, PB * k + PB : PB * k + 2 * PB], PB - off, 1)
                t = jnp.where(lanes(shape) < PB - off, t, n)
        picked = jnp.zeros((PB, PB), F32)
        for _ in range(3):
            part = t.astype(jnp.bfloat16)
            picked = picked + jnp.dot(one, part, preferred_element_type=F32)
            t = t - part.astype(F32)
        zs[h] = jnp.where(owned, picked, BIG)
    target = jnp.broadcast_to(selb[...], shape)
    nat = jnp.full(shape, BIG, F32)
    for k in range(CAP // PB):
        got = jnp.take_along_axis(
            wd[:, PB * k : PB * k + PB], target & (PB - 1), axis=1, mode="promise_in_bounds"
        )
        nat = jnp.where(target >> 7 == k, got, nat)
    bnat[0:ROWS, :] = jnp.where(row < count, nat, BIG)
    bnat[ROWS:PB, :] = jnp.full((PB - ROWS, PB), BIG, F32)
    for k, rows in enumerate(to_rows(bnat[...], ROWS // L)):
        b1r[pl.ds(first + L * k, L), :] = rows

    loads[2].wait()

    pl.semaphore_wait(barrier, H - 1 + NY - 1 + 8 + 9 - jnp.where(at_home, 1, 0))

    def remote(src, dst, ss, rs, c, h):
        return pltpu.make_async_remote_copy(
            src_ref=src, dst_ref=dst, send_sem=ss, recv_sem=rs, device_id=dev(c, h), device_id_type=MESH
        )

    mine = pl.ds(first, ROWS)
    partner = 2 * x + 1 - core

    def rows_of(h):
        return pl.ds(pl.multiple_of(h * ROWS, L), ROWS)

    def share(buf, ss, rs, n):
        to = partner if n == 0 else 2 * lax.rem(x + n, NX) + core
        return remote(buf.at[mine], buf.at[mine], ss.at[n], rs.at[n], cell, to)

    def pass_on(buf, ss, rs, n):
        part = buf.at[rows_of(2 * lax.rem(x - n + NX, NX) + core)]
        return remote(part, part, ss.at[n], rs.at[n], cell, partner)

    for n in (0, 1, 3, 2):
        share(b1r, s_b, r_b, n).start()

    def lend(n):
        chip = lax.rem(x + n, NX)
        return remote(zs.at[2 * chip + 1 - core], zq.at[n], s_zq.at[n], r_zq.at[n], cell, partner)

    def ship(n):
        chip = lax.rem(x + n, NX)
        return remote(zs.at[2 * chip + core], za.at[n - 1], s_a.at[n], r_a.at[n], cell, 2 * chip + core)

    for n in (2, 1, 3, 0):
        lend(n).start()

    def widen_w(k, carry):
        t = wd[:, pl.ds(pl.multiple_of(k * PB, PB), PB)]
        for q in range(8):
            wexp[8 * k + q] = spread(t, q)
        return carry

    lax.fori_loop(0, CAP // PB, widen_w, 0)
    unit_row = lax.broadcasted_iota(jnp.int32, (PB, PB), 0)
    for g in range(8):
        units[:, PB * g : PB * g + PB] = jnp.where(
            unit_row == L * g + (lanes((PB, PB)) & (L - 1)), 1.0, 0.0
        ).astype(jnp.bfloat16)

    def clear(k, carry):
        accb[k] = jnp.full((L, SH, PB), BIG, F32)
        return carry

    lax.fori_loop(0, ROWS // SH, clear, 0)
    a_row = me * SH + lax.broadcasted_iota(jnp.int32, (SH, PB), 0)

    def widen_cut(n, carry):
        h, jj = n // 8, lax.rem(n, 8)
        j = slot_cell(h, jj)
        t = cutb[:, pl.ds(pl.multiple_of(j * PB, PB), PB)].astype(F32)
        cutf[h, jj] = jnp.where((lanes((SH, PB)) == a_row) & (cell == j), 0.0, t)
        return carry

    lax.fori_loop(0, 64, widen_cut, 0, unroll=4)

    for n in (2, 1, 3, 0):
        own = 2 * lax.rem(x + n, NX) + core
        pltpu.make_async_copy(zq.at[n], zq.at[n], r_zq.at[n]).wait()
        zs[own] = jnp.minimum(zs[own], zq[n])
        if n:
            ship(n).start()
    send_cut = [
        remote(cutf.at[peer(r)], cutr.at[me], s_cut.at[r], r_cut.at[r], cell, peer(r)) for r in range(1, H)
    ]
    for c in send_cut[0:4]:
        c.start()
    cutr[me] = cutf[me]

    def over_block(n, carry):
        m = lax.rem(n + 1, 3)
        hop = jnp.where(n < 2, 0, jnp.where(m == 0, 1, jnp.where(m == 1, 3, 2)))
        same = (n == 0) | ((n >= 2) & (n < 5))
        src = 2 * lax.rem(x - hop + NX, NX) + jnp.where(same, core, 1 - core)

        @pl.when((n >= 1) & (n < 5))
        def _():
            pltpu.make_async_copy(b1r.at[mine], b1r.at[mine], r_b.at[hop]).wait()

        @pl.when((n >= 2) & (n < 5))
        def _():
            pass_on(b1r, s_bf, r_bf, hop).start()

        @pl.when(n >= 5)
        def _():
            pltpu.make_async_copy(b1r.at[mine], b1r.at[mine], r_bf.at[hop]).wait()

        r0 = pl.multiple_of(src * ROWS, L)

        def rows_u(k, carry):
            u0 = pl.multiple_of(k * SH, SH)
            acc = [accb[k, s] for s in range(L)]
            for q in range(ROWS // L):
                e = wexp[src * (ROWS // L) + q, pl.ds(u0, SH), :]
                for s in range(L):
                    acc[s] = jnp.minimum(acc[s], e + b1r[pl.ds(r0 + (q * L + s), 1), :])
            for s in range(L):
                accb[k, s] = acc[s]
            return carry

        lax.fori_loop(0, ROWS // SH, rows_u, 0)
        return carry

    lax.fori_loop(0, H, over_block, 0)

    def finish(k, carry):
        u0 = pl.multiple_of(k * SH, SH)
        u = first + u0 + lax.broadcasted_iota(jnp.int32, (SH, PB), 0)
        bnat[pl.ds(u0, SH), :] = jnp.where(u < count, fold([accb[k, s] for s in range(L)]), BIG)
        return carry

    lax.fori_loop(0, ROWS // SH, finish, 0, unroll=True)
    for k, rows in enumerate(to_rows(bnat[...], ROWS // L)):
        b2r[pl.ds(first + L * k, L), :] = rows
    for n in (1, 3, 2, 0):
        share(b2r, s_c, r_c, n).start()

    got = zs[me]
    for n in (1, 3, 2):
        pltpu.make_async_copy(za.at[n - 1], za.at[n - 1], r_a.at[n]).wait()
        got = jnp.minimum(got, za[n - 1])
    col = first + lanes((PB, PB))
    a1[...] = jnp.where(col < count, got, BIG)

    def strip(chip, cc):
        return pl.ds(pl.multiple_of((2 * chip + cc) * SH, SH), SH)

    def cross(i, chip):
        return remote(a2p.at[strip(chip, 1 - core)], a2q.at[i], s_q.at[i], r_q.at[i], cell, partner)

    def merged(i):
        chip = lax.rem(x + 1 + i, NX)
        at = strip(chip, core)
        pltpu.make_async_copy(a2q.at[i], a2q.at[i], r_q.at[i]).wait()
        a2p[at, :] = jnp.minimum(a2p[at, :], a2q[i])
        return remote(a2p.at[at], a2r.at[i], s_p.at[i], r_p.at[i], cell, 2 * chip + core)

    def from_chosen(i, carry):
        chip = lax.rem(x + 1 + i, NX)
        s0 = pl.multiple_of(chip * 2 * SH, 2 * SH)
        left = a1[pl.ds(s0, 2 * SH), :]

        acc = jnp.full((2 * SH, CAP), BIG, F32)
        for w in range(ROWS):
            acc = jnp.minimum(acc, left[:, w : w + 1] + wd[w : w + 1, :])
        a2p[pl.ds(s0, 2 * SH), :] = acc
        cross(i, chip).start()

        @pl.when(i >= 1)
        def _():
            merged(i - 1).start()

        return carry

    lax.fori_loop(0, NX, from_chosen, 0)

    for n in (1, 3, 2):
        pltpu.make_async_copy(b2r.at[mine], b2r.at[mine], r_c.at[n]).wait()
        pass_on(b2r, s_cf, r_cf, n).start()
    for c in send_cut[4:]:
        c.start()
    def contract(expanded, rows, groups):
        def step(k, acc):
            acc = list(acc)
            for q in range(8):
                e = expanded(8 * k + q)
                for s in range(L):
                    acc[s] = jnp.minimum(acc[s], e + rows(k * PB, q * L + s))
            return tuple(acc)

        acc = tuple(jnp.full((SH, PB), BIG, F32) for _ in range(L))
        return fold(list(lax.fori_loop(0, groups // 8, step, acc)))

    for n in range(NX - 1):
        pltpu.make_async_copy(a2r.at[n], a2r.at[n], r_p.at[n]).wait()
    pltpu.make_async_copy(a2q.at[NX - 1], a2q.at[NX - 1], r_q.at[NX - 1]).wait()
    best = jnp.minimum(a2p[strip(x, core), :], a2q[NX - 1])
    for n in range(NX - 1):
        best = jnp.minimum(best, a2r[n])
    a2c[...] = best
    for g in range(G):
        k, q = g // 8, g % 8
        a2exp[g] = spread(a2c[:, PB * k : PB * k + PB], q)
    pltpu.make_async_copy(b2r.at[mine], b2r.at[mine], r_c.at[0]).wait()
    for n in (1, 3, 2):
        pltpu.make_async_copy(b2r.at[mine], b2r.at[mine], r_cf.at[n]).wait()
    bnat[0:SH, :] = contract(lambda g: a2exp[g], lambda r0, r: b2r[pl.ds(pl.multiple_of(r0, PB) + r, 1), :], G)
    piece[...] = to_rows(bnat[...], 1)[0]

    b_own = z // 8
    slot_own = 2 * y + b_own
    mine_ch = ch.at[slot_own, pl.ds(pl.multiple_of(me * L, L), L)]

    def to_home(r):
        return remote(piece, mine_ch, s_z.at[r + 4], r_z.at[b_own * H + me], along(z + r) * NY + y, home)

    for r in (4, -4, 3, -3, 2, -2, 1, -1):
        to_home(r).start()

    @pl.when(home != me)
    def _():
        to_home(0).start()

    @pl.when(home == me)
    def _():
        pltpu.make_async_copy(piece, mine_ch, r_z.at[b_own * H + me]).start()

    for c in send_cut:
        c.wait()

    def widen(src, carry):
        t = cutr[src].reshape(PB, PB).astype(jnp.bfloat16)
        wide = jnp.dot(t, units[...], preferred_element_type=F32)
        for g in range(8):
            cutexp[src, g] = wide[:, PB * g : PB * g + PB]
        return carry

    lax.fori_loop(0, H, widen, 0)

    def from_source(yy, b):
        return along(z - (4 * (core + 2 * b) + lax.rem(x - yy + 4, 4)))

    def near(yy):
        return jnp.where(is_near(from_source(yy, 0)), 0, 1)

    def forward(jj, b, r):
        n = b * 8 + r + 3
        return remote(ch.at[jj], ch.at[jj], s_f.at[n], r_f.at[b], along(z + r) * NY + y, me)

    def parent(jj):
        def one(src, carry):
            got = contract_few(src)
            outb[jj, src] = got * SCALE
            return carry

        def contract_few(src):
            acc = [None] * L
            for g in range(8):
                e = cutexp[src, g, pl.ds(pl.multiple_of(jj * SH, SH), SH), :]
                for s in range(L):
                    sums = e + ch[jj, pl.ds(g * L + s, 1), :]
                    acc[s] = jnp.minimum(acc[s], sums) if g else sums
            return fold(acc)

        lax.fori_loop(0, H, one, 0, unroll=4)
        yy, b = jj // 2, lax.rem(jj, 2)
        j = (4 * (core + 2 * b) + lax.rem(x - yy + 4, 4)) * NY + yy
        where = o_ref.at[:, pl.ds(pl.multiple_of(j * PB, PB), PB)]
        for r in range(1, H):
            remote(outb.at[jj, peer(r)], where, s_o.at[r], r_o.at[r], cell, peer(r)).start()
        pltpu.make_async_copy(outb.at[jj, me], where, l_o).start()

    def along_y(r, jj, which):
        sem = which * NY + r
        return remote(ch.at[jj], ch.at[jj], s_y.at[sem], r_y.at[sem], z * NY + lax.rem(y + r, NY), me)

    def take(b, which):
        jj = 2 * y + b
        d = from_source(y, b)

        @pl.when(is_near(d))
        def _():
            for g in range(H):
                part = ch.at[jj, pl.ds(g * L, L)]
                pltpu.make_async_copy(part, part, r_z.at[b * H + g]).wait()

        @pl.when(jnp.logical_not(is_near(d)))
        def _():
            pltpu.make_async_copy(ch.at[jj], ch.at[jj], r_f.at[b]).wait()

        @pl.when(d == 4)
        def _():
            for k in (4, 3, 2, 1):
                forward(jj, b, k).start()

        @pl.when(d == NZ - 4)
        def _():
            for k in (3, 2, 1):
                forward(jj, b, -k).start()

        for k in (1, 3, 2):
            along_y(k, jj, which).start()

    b_near = near(y)
    both_near = is_near(from_source(y, 1 - b_near))

    def serve(n, carry):
        which, m = n // NY, lax.rem(n, NY)
        r = jnp.where(m >= 2, 5 - m, m)
        yy = lax.rem(y - r + NY, NY)
        first_b = near(yy)
        b = jnp.where(which == 0, first_b, 1 - first_b)
        jj = 2 * yy + b

        @pl.when(n == 0)
        def _():
            take(b_near, 0)

        @pl.when(((n == 0) & both_near) | ((n == NY) & jnp.logical_not(both_near)))
        def _():
            take(1 - b_near, 1)

        @pl.when(r > 0)
        def _():
            pltpu.make_async_copy(ch.at[jj], ch.at[jj], r_y.at[which * NY + r]).wait()

        parent(jj)
        return carry

    lax.fori_loop(0, 8, serve, 0)

    for n in range(NX):
        pltpu.make_async_copy(a2q.at[0], a2q.at[0], s_q.at[n]).wait()
        if n < NX - 1:
            pltpu.make_async_copy(a2q.at[0], a2q.at[0], s_p.at[n]).wait()
    for n in range(NX):
        lend(n).wait_send()
        share(b1r, s_b, r_b, n).wait_send()
        share(b2r, s_c, r_c, n).wait_send()
        if n:
            ship(n).wait_send()
            pass_on(b1r, s_bf, r_bf, n).wait_send()
            pass_on(b2r, s_cf, r_cf, n).wait_send()
    for r in range(-4, 5):
        if r:
            to_home(r).wait_send()

    @pl.when(home != me)
    def _():
        to_home(0).wait_send()

    for b in range(2):
        d = from_source(y, b)

        @pl.when(d == 4)
        def _(b=b):
            for k in range(1, 5):
                forward(2 * y + b, b, k).wait_send()

        @pl.when(d == NZ - 4)
        def _(b=b):
            for k in range(1, 4):
                forward(2 * y + b, b, -k).wait_send()

    for which in range(2):
        for r in range(1, NY):
            along_y(r, 2 * y, which).wait_send()
    for r in range(1, H):
        pltpu.make_async_copy(cutf.at[0], cutf.at[0], s_o.at[r]).wait()
        pltpu.make_async_copy(cutf.at[0], cutf.at[0], r_o.at[r]).wait()
    pltpu.make_async_copy(cutf.at[0], cutf.at[0], l_o).wait()


def per_device(weights, counts, select, cut_weights):
    hbm = pl.BlockSpec(memory_space=pltpu.HBM)

    def hold(a):
        return pltpu.with_memory_space_constraint(a, pltpu.HBM)

    def v(*shape):
        return pltpu.VMEM(shape, F32)

    def sem(n):
        return pltpu.SemaphoreType.DMA((n,))

    out = pl.pallas_call(
        kernel,
        out_shape=jax.ShapeDtypeStruct((SH, NZ * NY * PB), F32),
        in_specs=[hbm, pl.BlockSpec(memory_space=pltpu.SMEM), hbm, hbm],
        out_specs=hbm,
        scratch_shapes=[
            v(ROWS, CAP),
            v(G, ROWS, PB),
            v(H, PB, PB),
            v(NX, PB, PB),
            v(NX - 1, PB, PB),
            v(PB, PB),
            v(CAP, PB),
            v(PB, PB),
            v(ROWS // SH, L, SH, PB),
            v(PB, CAP),
            v(NX, SH, CAP),
            v(NX - 1, SH, CAP),
            v(SH, CAP),
            v(G, SH, PB),
            v(CAP, PB),
            v(SH, PB),
            pltpu.VMEM((SH, NZ * NY * PB), jnp.bfloat16),
            pltpu.VMEM((1, PB), jnp.int32),
            pltpu.VMEM((PB, 8 * PB), jnp.bfloat16),
            v(H, 8, SH, PB),
            v(H, 8, SH, PB),
            v(H, 8, PB, PB),
            v(8, PB, PB),
            v(8, H, SH, PB),
            sem(NX), sem(NX), sem(NX), sem(NX), sem(NX), sem(NX), sem(NX), sem(NX), sem(NX), sem(NX), sem(NX), sem(NX), sem(NX), sem(NX), sem(NX), sem(NX),
            sem(H), sem(H), sem(9), sem(2 * H), sem(16), sem(2), sem(2 * NY), sem(2 * NY), sem(H), sem(H),
            pltpu.SemaphoreType.DMA, sem(3),
        ],
        compiler_params=pltpu.CompilerParams(
            collective_id=0, has_side_effects=True, vmem_limit_bytes=48 * 1024 * 1024
        ),
    )(hold(weights), counts, hold(select), hold(cut_weights))
    return out[None]


def solution(mesh):
    in_specs = (P("cell", "help", None), P("cell"), P("cell", None), P("cell", "help", None))
    return jax.shard_map(
        per_device, mesh=mesh, in_specs=in_specs, out_specs=P("cell", "help", None), check_vma=False
    )
```

```python
import jax
import jax.numpy as jnp
from jax import lax
from jax.experimental import pallas as pl
from jax.experimental.pallas import tpu as pltpu
from jax.sharding import PartitionSpec as P

F32 = jnp.float32
BIG = 1048576.0
SCALE = 0.00390625
NZ, NY, NX = 16, 4, 4
H = 8
CAP = 896
ROWS = 112
PB = 128
SH = 16
L = 16
G = CAP // L
MESH = pl.DeviceIdType.MESH


def slot_cell(h, jj):
    x, c, y, b = h // 2, lax.rem(h, 2), jj // 2, lax.rem(jj, 2)
    return (4 * (c + 2 * b) + lax.rem(x - y + 4, 4)) * NY + y


def lanes(shape):
    return lax.broadcasted_iota(jnp.int32, shape, 1)


def spread(tile, q):
    index = L * q + (lanes(tile.shape) & (L - 1))
    return jnp.take_along_axis(tile, index, axis=1, mode="promise_in_bounds")


def to_rows(block, count):
    turned = jnp.transpose(block)
    lane = lanes((L, PB))
    row = lax.broadcasted_iota(jnp.int32, (L, PB), 0)
    out = []
    for k in range(count):
        part = jnp.zeros((L, PB), F32)
        for q in range(PB // L):
            piece = turned[L * q : L * q + L, :]
            shift = (L * (q - k)) % PB
            if shift:
                piece = pltpu.roll(piece, shift, 1)
            part = jnp.where(lane >> 4 == q, piece, part)
        out.append(jnp.where((lane & (L - 1)) >= row, part, pltpu.roll(part, L, 1)))
    return out


def fold(parts):
    lane = lanes(parts[0].shape)
    d = L // 2
    while d:
        merged = []
        for s in range(d):
            mask = ((lane - s) & d) == 0
            a = jnp.where(mask, parts[s], parts[s + d])
            b = jnp.where(mask, parts[s + d], parts[s])
            merged.append(jnp.minimum(a, pltpu.roll(b, PB - d, 1)))
        parts = merged
        d //= 2
    return parts[0]


def kernel(
    w_ref, count_ref, selv_ref, cut_ref, o_ref,
    wd, wexp, zs, zq, za, a1, b1r, bnat, accb, a2p, a2q, a2r, a2c, a2exp, b2r, piece, cutb, selb, units, cutf, cutr, cutexp,
    ch, outb,
    s_zq, r_zq, s_a, r_a, s_b, r_b, s_bf, r_bf, s_q, r_q, s_p, r_p, s_c, r_c, s_cf, r_cf, s_cut, r_cut, s_z, r_z, s_f, r_f, s_y, r_y,
    s_o, r_o, l_o, l_in,
):
    cell = lax.axis_index("cell")
    me = lax.axis_index("help")
    z, y = cell // NY, cell % NY
    x, core = me // 2, me % 2
    home = 2 * ((z + y) % 4) + (z // 4) % 2
    at_home = home == me

    def dev(c, h):
        return {"cell": c, "help": h}

    def peer(r):
        return lax.rem(me + r, H)

    def source_z(b):
        return 4 * (core + 2 * b) + lax.rem(x - y + 4, 4)

    loads = [
        pltpu.make_async_copy(w_ref.at[0], wd, l_in.at[0]),
        pltpu.make_async_copy(selv_ref, selb, l_in.at[1]),
        pltpu.make_async_copy(cut_ref.at[0], cutb, l_in.at[2]),
    ]
    for c in loads:
        c.start()

    barrier = pltpu.get_barrier_semaphore()

    def greet(c, h):
        pl.semaphore_signal(barrier, inc=1, device_id=dev(c, h), device_id_type=MESH)

    def along(zz):
        return lax.rem(zz + NZ, NZ)

    def is_near(d):
        return (d <= 4) | (d >= NZ - 4)

    for b in range(2):
        sz = source_z(b)

        @pl.when(is_near(along(z - sz)))
        def _(sz=sz):
            for r in range(1, H):
                greet(sz * NY + y, peer(r))

        @pl.when(is_near(along(z - sz)) & (sz != z))
        def _(sz=sz):
            greet(sz * NY + y, me)

    for r in (4, 3, 2, 1):
        greet(along(z + r) * NY + y, me)
        greet(along(z - r) * NY + y, me)
    for r in range(1, NY):
        greet(z * NY + lax.rem(y + r, NY), me)
    for r in range(1, H):
        greet(cell, peer(r))

    first = me * ROWS
    shape = (ROWS, PB)
    row = first + lax.broadcasted_iota(jnp.int32, shape, 0)
    loads[0].wait()
    for k in range(CAP // PB):
        t = jnp.where(lanes(shape) + PB * k == row, 0.0, wd[:, PB * k : PB * k + PB])
        wd[:, PB * k : PB * k + PB] = t
    loads[1].wait()
    count = count_ref[0]
    spot = lax.broadcasted_iota(jnp.int32, (PB, PB), 0)
    held = (jnp.broadcast_to(selb[...], (PB, PB)) == first + spot) & (spot < ROWS)
    one = jnp.transpose(jnp.where(held, 1.0, 0.0))
    owned = jnp.max(one, axis=1, keepdims=True) > 0.5
    one = one[:, 0:ROWS].astype(jnp.bfloat16)
    for h in range(H):
        k, off = (ROWS * h) // PB, (ROWS * h) % PB
        t = wd[:, PB * k : PB * k + PB]
        if off:
            t = pltpu.roll(t, PB - off, 1)
            if off + ROWS > PB:
                n = pltpu.roll(wd[:, PB * k + PB : PB * k + 2 * PB], PB - off, 1)
                t = jnp.where(lanes(shape) < PB - off, t, n)
        picked = jnp.zeros((PB, PB), F32)
        for _ in range(3):
            part = t.astype(jnp.bfloat16)
            picked = picked + jnp.dot(one, part, preferred_element_type=F32)
            t = t - part.astype(F32)
        zs[h] = jnp.where(owned, picked, BIG)
    target = jnp.broadcast_to(selb[...], shape)
    nat = jnp.full(shape, BIG, F32)
    for k in range(CAP // PB):
        got = jnp.take_along_axis(
            wd[:, PB * k : PB * k + PB], target & (PB - 1), axis=1, mode="promise_in_bounds"
        )
        nat = jnp.where(target >> 7 == k, got, nat)
    bnat[0:ROWS, :] = jnp.where(row < count, nat, BIG)
    bnat[ROWS:PB, :] = jnp.full((PB - ROWS, PB), BIG, F32)
    for k, rows in enumerate(to_rows(bnat[...], ROWS // L)):
        b1r[pl.ds(first + L * k, L), :] = rows

    loads[2].wait()

    pl.semaphore_wait(barrier, H - 1 + NY - 1 + 8 + 9 - jnp.where(at_home, 1, 0))

    def remote(src, dst, ss, rs, c, h):
        return pltpu.make_async_remote_copy(
            src_ref=src, dst_ref=dst, send_sem=ss, recv_sem=rs, device_id=dev(c, h), device_id_type=MESH
        )

    mine = pl.ds(first, ROWS)
    partner = 2 * x + 1 - core

    def rows_of(h):
        return pl.ds(pl.multiple_of(h * ROWS, L), ROWS)

    def share(buf, ss, rs, n):
        to = partner if n == 0 else 2 * lax.rem(x + n, NX) + core
        return remote(buf.at[mine], buf.at[mine], ss.at[n], rs.at[n], cell, to)

    def pass_on(buf, ss, rs, n):
        part = buf.at[rows_of(2 * lax.rem(x - n + NX, NX) + core)]
        return remote(part, part, ss.at[n], rs.at[n], cell, partner)

    for n in (0, 1, 3, 2):
        share(b1r, s_b, r_b, n).start()

    def lend(n):
        chip = lax.rem(x + n, NX)
        return remote(zs.at[2 * chip + 1 - core], zq.at[n], s_zq.at[n], r_zq.at[n], cell, partner)

    def ship(n):
        chip = lax.rem(x + n, NX)
        return remote(zs.at[2 * chip + core], za.at[n - 1], s_a.at[n], r_a.at[n], cell, 2 * chip + core)

    for n in (2, 1, 3, 0):
        lend(n).start()

    def widen_w(k, carry):
        t = wd[:, pl.ds(pl.multiple_of(k * PB, PB), PB)]
        for q in range(8):
            wexp[8 * k + q] = spread(t, q)
        return carry

    lax.fori_loop(0, CAP // PB, widen_w, 0)
    unit_row = lax.broadcasted_iota(jnp.int32, (PB, PB), 0)
    for g in range(8):
        units[:, PB * g : PB * g + PB] = jnp.where(
            unit_row == L * g + (lanes((PB, PB)) & (L - 1)), 1.0, 0.0
        ).astype(jnp.bfloat16)

    def clear(k, carry):
        accb[k] = jnp.full((L, SH, PB), BIG, F32)
        return carry

    lax.fori_loop(0, ROWS // SH, clear, 0)
    a_row = me * SH + lax.broadcasted_iota(jnp.int32, (SH, PB), 0)

    def widen_cut(n, carry):
        h, jj = n // 8, lax.rem(n, 8)
        j = slot_cell(h, jj)
        t = cutb[:, pl.ds(pl.multiple_of(j * PB, PB), PB)].astype(F32)
        cutf[h, jj] = jnp.where((lanes((SH, PB)) == a_row) & (cell == j), 0.0, t)
        return carry

    lax.fori_loop(0, 64, widen_cut, 0, unroll=4)

    for n in (2, 1, 3, 0):
        own = 2 * lax.rem(x + n, NX) + core
        pltpu.make_async_copy(zq.at[n], zq.at[n], r_zq.at[n]).wait()
        zs[own] = jnp.minimum(zs[own], zq[n])
        if n:
            ship(n).start()
    send_cut = [
        remote(cutf.at[peer(r)], cutr.at[me], s_cut.at[r], r_cut.at[r], cell, peer(r)) for r in range(1, H)
    ]
    for c in send_cut[0:4]:
        c.start()
    cutr[me] = cutf[me]

    def over_block(n, carry):
        m = lax.rem(n + 1, 3)
        hop = jnp.where(n < 2, 0, jnp.where(m == 0, 1, jnp.where(m == 1, 3, 2)))
        same = (n == 0) | ((n >= 2) & (n < 5))
        src = 2 * lax.rem(x - hop + NX, NX) + jnp.where(same, core, 1 - core)

        @pl.when((n >= 1) & (n < 5))
        def _():
            pltpu.make_async_copy(b1r.at[mine], b1r.at[mine], r_b.at[hop]).wait()

        @pl.when((n >= 2) & (n < 5))
        def _():
            pass_on(b1r, s_bf, r_bf, hop).start()

        @pl.when(n >= 5)
        def _():
            pltpu.make_async_copy(b1r.at[mine], b1r.at[mine], r_bf.at[hop]).wait()

        r0 = pl.multiple_of(src * ROWS, L)

        def rows_u(k, carry):
            u0 = pl.multiple_of(k * SH, SH)
            acc = [accb[k, s] for s in range(L)]
            for q in range(ROWS // L):
                e = wexp[src * (ROWS // L) + q, pl.ds(u0, SH), :]
                for s in range(L):
                    acc[s] = jnp.minimum(acc[s], e + b1r[pl.ds(r0 + (q * L + s), 1), :])
            for s in range(L):
                accb[k, s] = acc[s]
            return carry

        lax.fori_loop(0, ROWS // SH, rows_u, 0)
        return carry

    lax.fori_loop(0, H, over_block, 0)

    def finish(k, carry):
        u0 = pl.multiple_of(k * SH, SH)
        u = first + u0 + lax.broadcasted_iota(jnp.int32, (SH, PB), 0)
        bnat[pl.ds(u0, SH), :] = jnp.where(u < count, fold([accb[k, s] for s in range(L)]), BIG)
        return carry

    lax.fori_loop(0, ROWS // SH, finish, 0, unroll=True)
    for k, rows in enumerate(to_rows(bnat[...], ROWS // L)):
        b2r[pl.ds(first + L * k, L), :] = rows
    for n in (1, 3, 2, 0):
        share(b2r, s_c, r_c, n).start()

    got = zs[me]
    for n in (1, 3, 2):
        pltpu.make_async_copy(za.at[n - 1], za.at[n - 1], r_a.at[n]).wait()
        got = jnp.minimum(got, za[n - 1])
    col = first + lanes((PB, PB))
    a1[...] = jnp.where(col < count, got, BIG)

    def strip(chip, cc):
        return pl.ds(pl.multiple_of((2 * chip + cc) * SH, SH), SH)

    def cross(i, chip):
        return remote(a2p.at[strip(chip, 1 - core)], a2q.at[i], s_q.at[i], r_q.at[i], cell, partner)

    def merged(i):
        chip = lax.rem(x + 1 + i, NX)
        at = strip(chip, core)
        pltpu.make_async_copy(a2q.at[i], a2q.at[i], r_q.at[i]).wait()
        a2p[at, :] = jnp.minimum(a2p[at, :], a2q[i])
        return remote(a2p.at[at], a2r.at[i], s_p.at[i], r_p.at[i], cell, 2 * chip + core)

    def from_chosen(i, carry):
        chip = lax.rem(x + 1 + i, NX)
        s0 = pl.multiple_of(chip * 2 * SH, 2 * SH)
        left = a1[pl.ds(s0, 2 * SH), :]

        acc = jnp.full((2 * SH, CAP), BIG, F32)
        for w in range(ROWS):
            acc = jnp.minimum(acc, left[:, w : w + 1] + wd[w : w + 1, :])
        a2p[pl.ds(s0, 2 * SH), :] = acc
        cross(i, chip).start()

        @pl.when(i >= 1)
        def _():
            merged(i - 1).start()

        return carry

    lax.fori_loop(0, NX, from_chosen, 0)

    for n in (1, 3, 2):
        pltpu.make_async_copy(b2r.at[mine], b2r.at[mine], r_c.at[n]).wait()
        pass_on(b2r, s_cf, r_cf, n).start()
    for c in send_cut[4:]:
        c.start()
    def contract(expanded, rows, groups):
        def step(k, acc):
            acc = list(acc)
            for q in range(8):
                e = expanded(8 * k + q)
                for s in range(L):
                    acc[s] = jnp.minimum(acc[s], e + rows(k * PB, q * L + s))
            return tuple(acc)

        acc = tuple(jnp.full((SH, PB), BIG, F32) for _ in range(L))
        return fold(list(lax.fori_loop(0, groups // 8, step, acc)))

    for n in range(NX - 1):
        pltpu.make_async_copy(a2r.at[n], a2r.at[n], r_p.at[n]).wait()
    pltpu.make_async_copy(a2q.at[NX - 1], a2q.at[NX - 1], r_q.at[NX - 1]).wait()
    best = jnp.minimum(a2p[strip(x, core), :], a2q[NX - 1])
    for n in range(NX - 1):
        best = jnp.minimum(best, a2r[n])
    a2c[...] = best
    for g in range(G):
        k, q = g // 8, g % 8
        a2exp[g] = spread(a2c[:, PB * k : PB * k + PB], q)
    pltpu.make_async_copy(b2r.at[mine], b2r.at[mine], r_c.at[0]).wait()
    for n in (1, 3, 2):
        pltpu.make_async_copy(b2r.at[mine], b2r.at[mine], r_cf.at[n]).wait()
    bnat[0:SH, :] = contract(lambda g: a2exp[g], lambda r0, r: b2r[pl.ds(pl.multiple_of(r0, PB) + r, 1), :], G)
    piece[...] = to_rows(bnat[...], 1)[0]

    b_own = z // 8
    slot_own = 2 * y + b_own
    mine_ch = ch.at[slot_own, pl.ds(pl.multiple_of(me * L, L), L)]

    def to_home(r):
        return remote(piece, mine_ch, s_z.at[r + 4], r_z.at[b_own * H + me], along(z + r) * NY + y, home)

    for r in (4, -4, 3, -3, 2, -2, 1, -1):
        to_home(r).start()

    @pl.when(home != me)
    def _():
        to_home(0).start()

    @pl.when(home == me)
    def _():
        pltpu.make_async_copy(piece, mine_ch, r_z.at[b_own * H + me]).start()

    for c in send_cut:
        c.wait()

    def widen(src, carry):
        t = cutr[src].reshape(PB, PB).astype(jnp.bfloat16)
        wide = jnp.dot(t, units[...], preferred_element_type=F32)
        for g in range(8):
            cutexp[src, g] = wide[:, PB * g : PB * g + PB]
        return carry

    lax.fori_loop(0, H, widen, 0)

    def from_source(yy, b):
        return along(z - (4 * (core + 2 * b) + lax.rem(x - yy + 4, 4)))

    def near(yy):
        return jnp.where(is_near(from_source(yy, 0)), 0, 1)

    def forward(jj, b, r):
        n = b * 8 + r + 3
        return remote(ch.at[jj], ch.at[jj], s_f.at[n], r_f.at[b], along(z + r) * NY + y, me)

    def parent(jj):
        def one(src, carry):
            got = contract_few(src)
            outb[jj, src] = got * SCALE
            return carry

        def contract_few(src):
            acc = [None] * L
            for g in range(8):
                e = cutexp[src, g, pl.ds(pl.multiple_of(jj * SH, SH), SH), :]
                for s in range(L):
                    sums = e + ch[jj, pl.ds(g * L + s, 1), :]
                    acc[s] = jnp.minimum(acc[s], sums) if g else sums
            return fold(acc)

        lax.fori_loop(0, H, one, 0, unroll=4)
        yy, b = jj // 2, lax.rem(jj, 2)
        j = (4 * (core + 2 * b) + lax.rem(x - yy + 4, 4)) * NY + yy
        where = o_ref.at[:, pl.ds(pl.multiple_of(j * PB, PB), PB)]
        for r in range(1, H):
            remote(outb.at[jj, peer(r)], where, s_o.at[r], r_o.at[r], cell, peer(r)).start()
        pltpu.make_async_copy(outb.at[jj, me], where, l_o).start()

    def along_y(r, jj, which):
        sem = which * NY + r
        return remote(ch.at[jj], ch.at[jj], s_y.at[sem], r_y.at[sem], z * NY + lax.rem(y + r, NY), me)

    def take(b, which):
        jj = 2 * y + b
        d = from_source(y, b)

        @pl.when(is_near(d))
        def _():
            for g in range(H):
                part = ch.at[jj, pl.ds(g * L, L)]
                pltpu.make_async_copy(part, part, r_z.at[b * H + g]).wait()

        @pl.when(jnp.logical_not(is_near(d)))
        def _():
            pltpu.make_async_copy(ch.at[jj], ch.at[jj], r_f.at[b]).wait()

        @pl.when(d == 4)
        def _():
            for k in (4, 3, 2, 1):
                forward(jj, b, k).start()

        @pl.when(d == NZ - 4)
        def _():
            for k in (3, 2, 1):
                forward(jj, b, -k).start()

        for k in (1, 3, 2):
            along_y(k, jj, which).start()

    b_near = near(y)
    both_near = is_near(from_source(y, 1 - b_near))

    def serve(n, carry):
        which, m = n // NY, lax.rem(n, NY)
        r = jnp.where(m >= 2, 5 - m, m)
        yy = lax.rem(y - r + NY, NY)
        first_b = near(yy)
        b = jnp.where(which == 0, first_b, 1 - first_b)
        jj = 2 * yy + b

        @pl.when(n == 0)
        def _():
            take(b_near, 0)

        @pl.when(r > 0)
        def _():
            pltpu.make_async_copy(ch.at[jj], ch.at[jj], r_y.at[which * NY + r]).wait()

        @pl.when(((n == 0) & both_near) | ((n == NY - 1) & jnp.logical_not(both_near)))
        def _():
            take(1 - b_near, 1)

        parent(jj)
        return carry

    lax.fori_loop(0, 8, serve, 0)

    for n in range(NX):
        pltpu.make_async_copy(a2q.at[0], a2q.at[0], s_q.at[n]).wait()
        if n < NX - 1:
            pltpu.make_async_copy(a2q.at[0], a2q.at[0], s_p.at[n]).wait()
    for n in range(NX):
        lend(n).wait_send()
        share(b1r, s_b, r_b, n).wait_send()
        share(b2r, s_c, r_c, n).wait_send()
        if n:
            ship(n).wait_send()
            pass_on(b1r, s_bf, r_bf, n).wait_send()
            pass_on(b2r, s_cf, r_cf, n).wait_send()
    for r in range(-4, 5):
        if r:
            to_home(r).wait_send()

    @pl.when(home != me)
    def _():
        to_home(0).wait_send()

    for b in range(2):
        d = from_source(y, b)

        @pl.when(d == 4)
        def _(b=b):
            for k in range(1, 5):
                forward(2 * y + b, b, k).wait_send()

        @pl.when(d == NZ - 4)
        def _(b=b):
            for k in range(1, 4):
                forward(2 * y + b, b, -k).wait_send()

    for which in range(2):
        for r in range(1, NY):
            along_y(r, 2 * y, which).wait_send()
    for r in range(1, H):
        pltpu.make_async_copy(cutf.at[0], cutf.at[0], s_o.at[r]).wait()
        pltpu.make_async_copy(cutf.at[0], cutf.at[0], r_o.at[r]).wait()
    pltpu.make_async_copy(cutf.at[0], cutf.at[0], l_o).wait()


def per_device(weights, counts, select, cut_weights):
    hbm = pl.BlockSpec(memory_space=pltpu.HBM)

    def hold(a):
        return pltpu.with_memory_space_constraint(a, pltpu.HBM)

    def v(*shape):
        return pltpu.VMEM(shape, F32)

    def sem(n):
        return pltpu.SemaphoreType.DMA((n,))

    out = pl.pallas_call(
        kernel,
        out_shape=jax.ShapeDtypeStruct((SH, NZ * NY * PB), F32),
        in_specs=[hbm, pl.BlockSpec(memory_space=pltpu.SMEM), hbm, hbm],
        out_specs=hbm,
        scratch_shapes=[
            v(ROWS, CAP),
            v(G, ROWS, PB),
            v(H, PB, PB),
            v(NX, PB, PB),
            v(NX - 1, PB, PB),
            v(PB, PB),
            v(CAP, PB),
            v(PB, PB),
            v(ROWS // SH, L, SH, PB),
            v(PB, CAP),
            v(NX, SH, CAP),
            v(NX - 1, SH, CAP),
            v(SH, CAP),
            v(G, SH, PB),
            v(CAP, PB),
            v(SH, PB),
            pltpu.VMEM((SH, NZ * NY * PB), jnp.bfloat16),
            pltpu.VMEM((1, PB), jnp.int32),
            pltpu.VMEM((PB, 8 * PB), jnp.bfloat16),
            v(H, 8, SH, PB),
            v(H, 8, SH, PB),
            v(H, 8, PB, PB),
            v(8, PB, PB),
            v(8, H, SH, PB),
            sem(NX), sem(NX), sem(NX), sem(NX), sem(NX), sem(NX), sem(NX), sem(NX), sem(NX), sem(NX), sem(NX), sem(NX), sem(NX), sem(NX), sem(NX), sem(NX),
            sem(H), sem(H), sem(9), sem(2 * H), sem(16), sem(2), sem(2 * NY), sem(2 * NY), sem(H), sem(H),
            pltpu.SemaphoreType.DMA, sem(3),
        ],
        compiler_params=pltpu.CompilerParams(
            collective_id=0, has_side_effects=True, vmem_limit_bytes=48 * 1024 * 1024
        ),
    )(hold(weights), counts, hold(select), hold(cut_weights))
    return out[None]


def solution(mesh):
    in_specs = (P("cell", "help", None), P("cell"), P("cell", None), P("cell", "help", None))
    return jax.shard_map(
        per_device, mesh=mesh, in_specs=in_specs, out_specs=P("cell", "help", None), check_vma=False
    )
```

```python
import jax
import jax.numpy as jnp
from jax import lax
from jax.experimental import pallas as pl
from jax.experimental.pallas import tpu as pltpu
from jax.sharding import PartitionSpec as P

F32 = jnp.float32
BIG = 1048576.0
SCALE = 0.00390625
NZ, NY, NX = 16, 4, 4
H = 8
CAP = 896
ROWS = 112
PB = 128
SH = 16
L = 16
G = CAP // L
MESH = pl.DeviceIdType.MESH


def slot_cell(h, jj):
    x, c, y, b = h // 2, lax.rem(h, 2), jj // 2, lax.rem(jj, 2)
    return (4 * (c + 2 * b) + lax.rem(x - y + 4, 4)) * NY + y


def lanes(shape):
    return lax.broadcasted_iota(jnp.int32, shape, 1)


def spread(tile, q):
    index = L * q + (lanes(tile.shape) & (L - 1))
    return jnp.take_along_axis(tile, index, axis=1, mode="promise_in_bounds")


def to_rows(block, count):
    turned = jnp.transpose(block)
    lane = lanes((L, PB))
    row = lax.broadcasted_iota(jnp.int32, (L, PB), 0)
    out = []
    for k in range(count):
        part = jnp.zeros((L, PB), F32)
        for q in range(PB // L):
            piece = turned[L * q : L * q + L, :]
            shift = (L * (q - k)) % PB
            if shift:
                piece = pltpu.roll(piece, shift, 1)
            part = jnp.where(lane >> 4 == q, piece, part)
        out.append(jnp.where((lane & (L - 1)) >= row, part, pltpu.roll(part, L, 1)))
    return out


def fold(parts):
    lane = lanes(parts[0].shape)
    d = L // 2
    while d:
        merged = []
        for s in range(d):
            mask = ((lane - s) & d) == 0
            a = jnp.where(mask, parts[s], parts[s + d])
            b = jnp.where(mask, parts[s + d], parts[s])
            merged.append(jnp.minimum(a, pltpu.roll(b, PB - d, 1)))
        parts = merged
        d //= 2
    return parts[0]


def kernel(
    w_ref, count_ref, selv_ref, cut_ref, o_ref,
    wd, wexp, zs, zq, za, a1, b1r, bnat, accb, a2p, a2q, a2r, a2c, a2exp, b2r, piece, cutb, selb, units, cutf, cutr, cutexp,
    ch, outb,
    s_zq, r_zq, s_a, r_a, s_b, r_b, s_bf, r_bf, s_q, r_q, s_p, r_p, s_c, r_c, s_cf, r_cf, s_cut, r_cut, s_z, r_z, s_f, r_f, s_y, r_y,
    s_o, r_o, l_o, l_in,
):
    cell = lax.axis_index("cell")
    me = lax.axis_index("help")
    z, y = cell // NY, cell % NY
    x, core = me // 2, me % 2
    home = 2 * ((z + y) % 4) + (z // 4) % 2
    at_home = home == me

    def dev(c, h):
        return {"cell": c, "help": h}

    def peer(r):
        return lax.rem(me + r, H)

    def source_z(b):
        return 4 * (core + 2 * b) + lax.rem(x - y + 4, 4)

    loads = [
        pltpu.make_async_copy(w_ref.at[0], wd, l_in.at[0]),
        pltpu.make_async_copy(selv_ref, selb, l_in.at[1]),
        pltpu.make_async_copy(cut_ref.at[0], cutb, l_in.at[2]),
    ]
    for c in loads:
        c.start()

    barrier = pltpu.get_barrier_semaphore()

    def greet(c, h):
        pl.semaphore_signal(barrier, inc=1, device_id=dev(c, h), device_id_type=MESH)

    def along(zz):
        return lax.rem(zz + NZ, NZ)

    def is_near(d):
        return (d <= 4) | (d >= NZ - 4)

    for b in range(2):
        sz = source_z(b)

        @pl.when(is_near(along(z - sz)))
        def _(sz=sz):
            for r in range(1, H):
                greet(sz * NY + y, peer(r))

        @pl.when(is_near(along(z - sz)) & (sz != z))
        def _(sz=sz):
            greet(sz * NY + y, me)

    for r in (4, 3, 2, 1):
        greet(along(z + r) * NY + y, me)
        greet(along(z - r) * NY + y, me)
    for r in range(1, NY):
        greet(z * NY + lax.rem(y + r, NY), me)
    for r in range(1, H):
        greet(cell, peer(r))

    first = me * ROWS
    shape = (ROWS, PB)
    row = first + lax.broadcasted_iota(jnp.int32, shape, 0)
    loads[0].wait()
    for k in range(CAP // PB):
        t = jnp.where(lanes(shape) + PB * k == row, 0.0, wd[:, PB * k : PB * k + PB])
        wd[:, PB * k : PB * k + PB] = t
    loads[1].wait()
    count = count_ref[0]
    spot = lax.broadcasted_iota(jnp.int32, (PB, PB), 0)
    held = (jnp.broadcast_to(selb[...], (PB, PB)) == first + spot) & (spot < ROWS)
    one = jnp.transpose(jnp.where(held, 1.0, 0.0))
    owned = jnp.max(one, axis=1, keepdims=True) > 0.5
    one = one[:, 0:ROWS].astype(jnp.bfloat16)
    for h in range(H):
        k, off = (ROWS * h) // PB, (ROWS * h) % PB
        t = wd[:, PB * k : PB * k + PB]
        if off:
            t = pltpu.roll(t, PB - off, 1)
            if off + ROWS > PB:
                n = pltpu.roll(wd[:, PB * k + PB : PB * k + 2 * PB], PB - off, 1)
                t = jnp.where(lanes(shape) < PB - off, t, n)
        picked = jnp.zeros((PB, PB), F32)
        for _ in range(3):
            part = t.astype(jnp.bfloat16)
            picked = picked + jnp.dot(one, part, preferred_element_type=F32)
            t = t - part.astype(F32)
        zs[h] = jnp.where(owned, picked, BIG)
    target = jnp.broadcast_to(selb[...], shape)
    nat = jnp.full(shape, BIG, F32)
    for k in range(CAP // PB):
        got = jnp.take_along_axis(
            wd[:, PB * k : PB * k + PB], target & (PB - 1), axis=1, mode="promise_in_bounds"
        )
        nat = jnp.where(target >> 7 == k, got, nat)
    bnat[0:ROWS, :] = jnp.where(row < count, nat, BIG)
    bnat[ROWS:PB, :] = jnp.full((PB - ROWS, PB), BIG, F32)
    for k, rows in enumerate(to_rows(bnat[...], ROWS // L)):
        b1r[pl.ds(first + L * k, L), :] = rows

    loads[2].wait()

    pl.semaphore_wait(barrier, H - 1 + NY - 1 + 8 + 9 - jnp.where(at_home, 1, 0))

    def remote(src, dst, ss, rs, c, h):
        return pltpu.make_async_remote_copy(
            src_ref=src, dst_ref=dst, send_sem=ss, recv_sem=rs, device_id=dev(c, h), device_id_type=MESH
        )

    mine = pl.ds(first, ROWS)
    partner = 2 * x + 1 - core

    def rows_of(h):
        return pl.ds(pl.multiple_of(h * ROWS, L), ROWS)

    def share(buf, ss, rs, n):
        to = partner if n == 0 else 2 * lax.rem(x + n, NX) + core
        return remote(buf.at[mine], buf.at[mine], ss.at[n], rs.at[n], cell, to)

    def pass_on(buf, ss, rs, n):
        part = buf.at[rows_of(2 * lax.rem(x - n + NX, NX) + core)]
        return remote(part, part, ss.at[n], rs.at[n], cell, partner)

    for n in (0, 1, 3, 2):
        share(b1r, s_b, r_b, n).start()

    def lend(n):
        chip = lax.rem(x + n, NX)
        return remote(zs.at[2 * chip + 1 - core], zq.at[n], s_zq.at[n], r_zq.at[n], cell, partner)

    def ship(n):
        chip = lax.rem(x + n, NX)
        return remote(zs.at[2 * chip + core], za.at[n - 1], s_a.at[n], r_a.at[n], cell, 2 * chip + core)

    for n in (2, 1, 3, 0):
        lend(n).start()

    def widen_w(k, carry):
        t = wd[:, pl.ds(pl.multiple_of(k * PB, PB), PB)]
        for q in range(8):
            wexp[8 * k + q] = spread(t, q)
        return carry

    lax.fori_loop(0, CAP // PB, widen_w, 0)
    unit_row = lax.broadcasted_iota(jnp.int32, (PB, PB), 0)
    for g in range(8):
        units[:, PB * g : PB * g + PB] = jnp.where(
            unit_row == L * g + (lanes((PB, PB)) & (L - 1)), 1.0, 0.0
        ).astype(jnp.bfloat16)

    def clear(k, carry):
        accb[k] = jnp.full((L, SH, PB), BIG, F32)
        return carry

    lax.fori_loop(0, ROWS // SH, clear, 0)
    a_row = me * SH + lax.broadcasted_iota(jnp.int32, (SH, PB), 0)

    def widen_cut(n, carry):
        h, jj = n // 8, lax.rem(n, 8)
        j = slot_cell(h, jj)
        t = cutb[:, pl.ds(pl.multiple_of(j * PB, PB), PB)].astype(F32)
        cutf[h, jj] = jnp.where((lanes((SH, PB)) == a_row) & (cell == j), 0.0, t)
        return carry

    lax.fori_loop(0, 64, widen_cut, 0, unroll=4)

    for n in (2, 1, 3, 0):
        own = 2 * lax.rem(x + n, NX) + core
        pltpu.make_async_copy(zq.at[n], zq.at[n], r_zq.at[n]).wait()
        zs[own] = jnp.minimum(zs[own], zq[n])
        if n:
            ship(n).start()
    send_cut = [
        remote(cutf.at[peer(r)], cutr.at[me], s_cut.at[r], r_cut.at[r], cell, peer(r)) for r in range(1, H)
    ]
    for c in send_cut[0:4]:
        c.start()
    cutr[me] = cutf[me]

    def over_block(n, carry):
        m = lax.rem(n + 1, 3)
        hop = jnp.where(n < 2, 0, jnp.where(m == 0, 1, jnp.where(m == 1, 3, 2)))
        same = (n == 0) | ((n >= 2) & (n < 5))
        src = 2 * lax.rem(x - hop + NX, NX) + jnp.where(same, core, 1 - core)

        @pl.when((n >= 1) & (n < 5))
        def _():
            pltpu.make_async_copy(b1r.at[mine], b1r.at[mine], r_b.at[hop]).wait()

        @pl.when((n >= 2) & (n < 5))
        def _():
            pass_on(b1r, s_bf, r_bf, hop).start()

        @pl.when(n >= 5)
        def _():
            pltpu.make_async_copy(b1r.at[mine], b1r.at[mine], r_bf.at[hop]).wait()

        r0 = pl.multiple_of(src * ROWS, L)

        def rows_u(k, carry):
            u0 = pl.multiple_of(k * SH, SH)
            acc = [accb[k, s] for s in range(L)]
            for q in range(ROWS // L):
                e = wexp[src * (ROWS // L) + q, pl.ds(u0, SH), :]
                for s in range(L):
                    acc[s] = jnp.minimum(acc[s], e + b1r[pl.ds(r0 + (q * L + s), 1), :])
            for s in range(L):
                accb[k, s] = acc[s]
            return carry

        lax.fori_loop(0, ROWS // SH, rows_u, 0)
        return carry

    lax.fori_loop(0, H, over_block, 0)

    def finish(k, carry):
        u0 = pl.multiple_of(k * SH, SH)
        u = first + u0 + lax.broadcasted_iota(jnp.int32, (SH, PB), 0)
        bnat[pl.ds(u0, SH), :] = jnp.where(u < count, fold([accb[k, s] for s in range(L)]), BIG)
        return carry

    lax.fori_loop(0, ROWS // SH, finish, 0, unroll=True)
    for k, rows in enumerate(to_rows(bnat[...], ROWS // L)):
        b2r[pl.ds(first + L * k, L), :] = rows
    for n in (1, 3, 2, 0):
        share(b2r, s_c, r_c, n).start()

    got = zs[me]
    for n in (1, 3, 2):
        pltpu.make_async_copy(za.at[n - 1], za.at[n - 1], r_a.at[n]).wait()
        got = jnp.minimum(got, za[n - 1])
    col = first + lanes((PB, PB))
    a1[...] = jnp.where(col < count, got, BIG)

    def strip(chip, cc):
        return pl.ds(pl.multiple_of((2 * chip + cc) * SH, SH), SH)

    def cross(i, chip):
        return remote(a2p.at[strip(chip, 1 - core)], a2q.at[i], s_q.at[i], r_q.at[i], cell, partner)

    def merged(i):
        chip = lax.rem(x + 1 + i, NX)
        at = strip(chip, core)
        pltpu.make_async_copy(a2q.at[i], a2q.at[i], r_q.at[i]).wait()
        a2p[at, :] = jnp.minimum(a2p[at, :], a2q[i])
        return remote(a2p.at[at], a2r.at[i], s_p.at[i], r_p.at[i], cell, 2 * chip + core)

    def from_chosen(i, carry):
        chip = lax.rem(x + 1 + i, NX)
        s0 = pl.multiple_of(chip * 2 * SH, 2 * SH)
        left = a1[pl.ds(s0, 2 * SH), :]

        acc = jnp.full((2 * SH, CAP), BIG, F32)
        for w in range(ROWS):
            acc = jnp.minimum(acc, left[:, w : w + 1] + wd[w : w + 1, :])
        a2p[pl.ds(s0, 2 * SH), :] = acc
        cross(i, chip).start()

        @pl.when(i >= 1)
        def _():
            merged(i - 1).start()

        return carry

    lax.fori_loop(0, NX, from_chosen, 0)

    for n in (1, 3, 2):
        pltpu.make_async_copy(b2r.at[mine], b2r.at[mine], r_c.at[n]).wait()
        pass_on(b2r, s_cf, r_cf, n).start()
    for c in send_cut[4:]:
        c.start()
    def contract(expanded, rows, groups):
        def step(k, acc):
            acc = list(acc)
            for q in range(8):
                e = expanded(8 * k + q)
                for s in range(L):
                    acc[s] = jnp.minimum(acc[s], e + rows(k * PB, q * L + s))
            return tuple(acc)

        acc = tuple(jnp.full((SH, PB), BIG, F32) for _ in range(L))
        return fold(list(lax.fori_loop(0, groups // 8, step, acc)))

    for n in range(NX - 1):
        pltpu.make_async_copy(a2r.at[n], a2r.at[n], r_p.at[n]).wait()
    pltpu.make_async_copy(a2q.at[NX - 1], a2q.at[NX - 1], r_q.at[NX - 1]).wait()
    best = jnp.minimum(a2p[strip(x, core), :], a2q[NX - 1])
    for n in range(NX - 1):
        best = jnp.minimum(best, a2r[n])
    a2c[...] = best
    for g in range(G):
        k, q = g // 8, g % 8
        a2exp[g] = spread(a2c[:, PB * k : PB * k + PB], q)
    pltpu.make_async_copy(b2r.at[mine], b2r.at[mine], r_c.at[0]).wait()
    for n in (1, 3, 2):
        pltpu.make_async_copy(b2r.at[mine], b2r.at[mine], r_cf.at[n]).wait()
    bnat[0:SH, :] = contract(lambda g: a2exp[g], lambda r0, r: b2r[pl.ds(pl.multiple_of(r0, PB) + r, 1), :], G)
    piece[...] = to_rows(bnat[...], 1)[0]

    b_own = z // 8
    slot_own = 2 * y + b_own
    mine_ch = ch.at[slot_own, pl.ds(pl.multiple_of(me * L, L), L)]

    def to_home(r):
        return remote(piece, mine_ch, s_z.at[r + 4], r_z.at[b_own * H + me], along(z + r) * NY + y, home)

    for r in (4, -4, 3, -3, 2, -2, 1, -1):
        to_home(r).start()

    @pl.when(home != me)
    def _():
        to_home(0).start()

    @pl.when(home == me)
    def _():
        pltpu.make_async_copy(piece, mine_ch, r_z.at[b_own * H + me]).start()

    for c in send_cut:
        c.wait()

    def widen(src, carry):
        t = cutr[src].reshape(PB, PB).astype(jnp.bfloat16)
        wide = jnp.dot(t, units[...], preferred_element_type=F32)
        for g in range(8):
            cutexp[src, g] = wide[:, PB * g : PB * g + PB]
        return carry

    lax.fori_loop(0, H, widen, 0)

    def from_source(yy, b):
        return along(z - (4 * (core + 2 * b) + lax.rem(x - yy + 4, 4)))

    def near(yy):
        return jnp.where(is_near(from_source(yy, 0)), 0, 1)

    def forward(jj, b, r):
        n = b * 8 + r + 3
        return remote(ch.at[jj], ch.at[jj], s_f.at[n], r_f.at[b], along(z + r) * NY + y, me)

    def parent(jj):
        def one(src, carry):
            got = contract_few(src)
            outb[jj, src] = got * SCALE
            return carry

        def contract_few(src):
            acc = [None] * L
            for g in range(8):
                e = cutexp[src, g, pl.ds(pl.multiple_of(jj * SH, SH), SH), :]
                for s in range(L):
                    sums = e + ch[jj, pl.ds(g * L + s, 1), :]
                    acc[s] = jnp.minimum(acc[s], sums) if g else sums
            return fold(acc)

        lax.fori_loop(0, H, one, 0, unroll=4)
        yy, b = jj // 2, lax.rem(jj, 2)
        j = (4 * (core + 2 * b) + lax.rem(x - yy + 4, 4)) * NY + yy
        where = o_ref.at[:, pl.ds(pl.multiple_of(j * PB, PB), PB)]
        for r in range(1, H):
            remote(outb.at[jj, peer(r)], where, s_o.at[r], r_o.at[r], cell, peer(r)).start()
        pltpu.make_async_copy(outb.at[jj, me], where, l_o).start()

    def along_y(r, jj, which):
        sem = which * NY + r
        return remote(ch.at[jj], ch.at[jj], s_y.at[sem], r_y.at[sem], z * NY + lax.rem(y + r, NY), me)

    def take(b, which):
        jj = 2 * y + b
        d = from_source(y, b)

        @pl.when(is_near(d))
        def _():
            for g in range(H):
                part = ch.at[jj, pl.ds(g * L, L)]
                pltpu.make_async_copy(part, part, r_z.at[b * H + g]).wait()

        @pl.when(jnp.logical_not(is_near(d)))
        def _():
            pltpu.make_async_copy(ch.at[jj], ch.at[jj], r_f.at[b]).wait()

        @pl.when(d == 4)
        def _():
            for k in (4, 3, 2, 1):
                forward(jj, b, k).start()

        @pl.when(d == NZ - 4)
        def _():
            for k in (3, 2, 1):
                forward(jj, b, -k).start()

        for k in (1, 3, 2):
            along_y(k, jj, which).start()

    b_near = near(y)
    both_near = is_near(from_source(y, 1 - b_near))

    def serve(n, carry):
        which, m = n // NY, lax.rem(n, NY)
        r = jnp.where(m >= 2, 5 - m, m)
        yy = lax.rem(y - r + NY, NY)
        first_b = near(yy)
        b = jnp.where(which == 0, first_b, 1 - first_b)
        jj = 2 * yy + b

        @pl.when(n == 0)
        def _():
            take(b_near, 0)

        @pl.when(r > 0)
        def _():
            pltpu.make_async_copy(ch.at[jj], ch.at[jj], r_y.at[which * NY + r]).wait()

        @pl.when(((n == 0) & both_near) | ((n == NY - 2) & jnp.logical_not(both_near)))
        def _():
            take(1 - b_near, 1)

        parent(jj)
        return carry

    lax.fori_loop(0, 8, serve, 0)

    for n in range(NX):
        pltpu.make_async_copy(a2q.at[0], a2q.at[0], s_q.at[n]).wait()
        if n < NX - 1:
            pltpu.make_async_copy(a2q.at[0], a2q.at[0], s_p.at[n]).wait()
    for n in range(NX):
        lend(n).wait_send()
        share(b1r, s_b, r_b, n).wait_send()
        share(b2r, s_c, r_c, n).wait_send()
        if n:
            ship(n).wait_send()
            pass_on(b1r, s_bf, r_bf, n).wait_send()
            pass_on(b2r, s_cf, r_cf, n).wait_send()
    for r in range(-4, 5):
        if r:
            to_home(r).wait_send()

    @pl.when(home != me)
    def _():
        to_home(0).wait_send()

    for b in range(2):
        d = from_source(y, b)

        @pl.when(d == 4)
        def _(b=b):
            for k in range(1, 5):
                forward(2 * y + b, b, k).wait_send()

        @pl.when(d == NZ - 4)
        def _(b=b):
            for k in range(1, 4):
                forward(2 * y + b, b, -k).wait_send()

    for which in range(2):
        for r in range(1, NY):
            along_y(r, 2 * y, which).wait_send()
    for r in range(1, H):
        pltpu.make_async_copy(cutf.at[0], cutf.at[0], s_o.at[r]).wait()
        pltpu.make_async_copy(cutf.at[0], cutf.at[0], r_o.at[r]).wait()
    pltpu.make_async_copy(cutf.at[0], cutf.at[0], l_o).wait()


def per_device(weights, counts, select, cut_weights):
    hbm = pl.BlockSpec(memory_space=pltpu.HBM)

    def hold(a):
        return pltpu.with_memory_space_constraint(a, pltpu.HBM)

    def v(*shape):
        return pltpu.VMEM(shape, F32)

    def sem(n):
        return pltpu.SemaphoreType.DMA((n,))

    out = pl.pallas_call(
        kernel,
        out_shape=jax.ShapeDtypeStruct((SH, NZ * NY * PB), F32),
        in_specs=[hbm, pl.BlockSpec(memory_space=pltpu.SMEM), hbm, hbm],
        out_specs=hbm,
        scratch_shapes=[
            v(ROWS, CAP),
            v(G, ROWS, PB),
            v(H, PB, PB),
            v(NX, PB, PB),
            v(NX - 1, PB, PB),
            v(PB, PB),
            v(CAP, PB),
            v(PB, PB),
            v(ROWS // SH, L, SH, PB),
            v(PB, CAP),
            v(NX, SH, CAP),
            v(NX - 1, SH, CAP),
            v(SH, CAP),
            v(G, SH, PB),
            v(CAP, PB),
            v(SH, PB),
            pltpu.VMEM((SH, NZ * NY * PB), jnp.bfloat16),
            pltpu.VMEM((1, PB), jnp.int32),
            pltpu.VMEM((PB, 8 * PB), jnp.bfloat16),
            v(H, 8, SH, PB),
            v(H, 8, SH, PB),
            v(H, 8, PB, PB),
            v(8, PB, PB),
            v(8, H, SH, PB),
            sem(NX), sem(NX), sem(NX), sem(NX), sem(NX), sem(NX), sem(NX), sem(NX), sem(NX), sem(NX), sem(NX), sem(NX), sem(NX), sem(NX), sem(NX), sem(NX),
            sem(H), sem(H), sem(9), sem(2 * H), sem(16), sem(2), sem(2 * NY), sem(2 * NY), sem(H), sem(H),
            pltpu.SemaphoreType.DMA, sem(3),
        ],
        compiler_params=pltpu.CompilerParams(
            collective_id=0, has_side_effects=True, vmem_limit_bytes=48 * 1024 * 1024
        ),
    )(hold(weights), counts, hold(select), hold(cut_weights))
    return out[None]


def solution(mesh):
    in_specs = (P("cell", "help", None), P("cell"), P("cell", None), P("cell", "help", None))
    return jax.shard_map(
        per_device, mesh=mesh, in_specs=in_specs, out_specs=P("cell", "help", None), check_vma=False
    )
```
